32 devices in a mesh: dp: 32 (over z, y, x, core).
Axes of the slice: x: 2, y: 2, z: 4, core: 2. Of those that a mesh axis runs over, the one named last changes fastest.
Arguments:
- grads: bfloat16 [64, 1024, 1024], P('dp'), may hold values from -6 to 6
- memory: bfloat16 [64, 1024, 1024], P('dp'), may hold values from -6 to 6
- block_ids: int32 [16], replicated, may hold values from 0 to 63, as said below
- layer_ids: int32 [16], replicated, may hold values from 0 to 1, as said below
- master: float32 [128, 16384], P(None, 'dp'), may hold values from -8 to 8
- first_moment: float32 [128, 16384], P(None, 'dp'), may hold values from -8 to 8
- second_moment: float32 [128, 16384], P(None, 'dp'), may hold values from 0.25 to 4
Outputs:
- new_memory: bfloat16 [64, 1024, 1024], P('dp')
- master_new: float32 [128, 16384], P(None, 'dp')
- first_new: float32 [128, 16384], P(None, 'dp')
- second_new: float32 [128, 16384], P(None, 'dp')
- step_blocks: bfloat16 [16, 16384], replicated
The draws below stay inside these ranges and needn't reach their ends.
Inputs may be any that keep to these rules, and one draw needn't show every extreme that they name: Block ids number the 64 tiles of a layer, and the pairs (layer_ids[k], block_ids[k]) are distinct. `layer_ids`: every layer is named by at least a quarter of the 16 entries, rounded down.
All inputs are finite; a program needn't handle non-finite values.
Results may differ from the reference program's by a relative error of at most 0.0004.
Values may be sent and summed in bfloat16 or wider, within the bound.
A program may use at most 64 MiB of HBM per device.

```python
import math
import jax
import jax.numpy as jnp
from jax import lax

D = 1024
LAYERS = 2
TILE = 128
SEL = 16
BLOCKS_LAYER = 64
BLOCKS = 128
TILE_ENT = 16384
N_DP = 32


def pick_entries(key):
    folded = jax.random.fold_in(key, 7)
    key_count, key_first, key_second, key_shuffle = jax.random.split(folded, 4)
    least = SEL // 4
    count_first = jax.random.randint(key_count, (), least, SEL - least + 1)
    first_perm = jax.random.permutation(key_first, BLOCKS_LAYER)[:SEL]
    second_perm = jax.random.permutation(key_second, BLOCKS_LAYER)[:SEL]
    position = jnp.arange(SEL, dtype=jnp.int32)
    layer_list = (position >= count_first).astype(jnp.int32)
    later_index = jnp.clip(position - count_first, 0, SEL - 1)
    block_list = jnp.where(layer_list == 0, first_perm[position], second_perm[later_index]).astype(jnp.int32)
    shuffle = jax.random.permutation(key_shuffle, SEL)
    return (layer_list[shuffle], block_list[shuffle])


def draw_block_ids(key, part):
    return pick_entries(key)[1]


def draw_layer_ids(key, part):
    return pick_entries(key)[0]


def rising_field(key):
    entry_row = (jnp.arange(TILE_ENT) // TILE).astype(jnp.float32)
    factor = 1.0 + 2.0 * entry_row / (TILE - 1)
    normal_part = jnp.clip(jax.random.normal(key, (BLOCKS, TILE_ENT), jnp.float32), -4.0, 4.0)
    return normal_part * factor[None, :] * 0.5


def draw_master(key, part):
    return rising_field(jax.random.fold_in(key, 11))


def draw_first_moment(key, part):
    return rising_field(jax.random.fold_in(key, 23))


def shard_levels(key, shape, shards, smallest, high):
    def one(axis_at, parts):
        heights = jax.random.uniform(jax.random.fold_in(jax.random.fold_in(key, 6), axis_at), (parts,), jnp.float32, smallest / len(shards), high / len(shards))
        return jnp.repeat(jnp.exp(heights), shape[axis_at] // parts).reshape((-1,) + (1,) * (len(shape) - axis_at - 1))

    gain = one(*shards[0])
    for cut in shards[1:]:
        gain = gain * one(*cut)
    return gain


def scatter_about(rng, extent, deviation, limit, cuts=(), kind=jnp.bfloat16):
    loudness = shard_levels(rng, extent, cuts, -0.22, 0.18) if cuts else 1.0
    entries = jax.random.normal(rng, extent, jnp.float32) * deviation * loudness
    return jnp.minimum(jnp.maximum(entries, -limit), limit).astype(kind)


def setup_inputs(seed: int = 0) -> dict:
    seeds = jax.random.split(jax.random.key(seed), 8)
    return {
        "grads": scatter_about(seeds[0], (N_DP * LAYERS, D, D), 0.5, 6.0, ((0, 32),)),
        "memory": scatter_about(seeds[1], (N_DP * LAYERS, D, D), 0.5, 6.0, ((0, 32),)),
        "block_ids": draw_block_ids(jax.random.fold_in(seeds[7], 71), 0),
        "layer_ids": draw_layer_ids(jax.random.fold_in(seeds[7], 71), 0),
        "master": draw_master(jax.random.fold_in(seeds[7], 71), 0),
        "first_moment": draw_first_moment(jax.random.fold_in(seeds[7], 71), 0),
        "second_moment": jnp.clip(jnp.exp(math.log(4.0) - 2.7725887 * jax.random.uniform(seeds[6], (BLOCKS, TILE_ENT), jnp.float32) ** shard_levels(seeds[6], (BLOCKS, TILE_ENT), ((1, 32),), -0.2, 0.2)), 0.25, 4.0),
    }


filter_rate = 0.3
beta_one = 0.9
beta_two = 0.999
adam_eps = 1e-06
weight_decay = 0.01
learn_rate = 0.01
norm_eps = 1e-06

def take_tiles(source, layer_ids, tile_row, tile_col):

    def single(layer_id, row_tile, col_tile):
        return lax.dynamic_slice(source, (layer_id, row_tile * TILE, col_tile * TILE), (1, TILE, TILE))[0]
    return jax.vmap(single)(layer_ids, tile_row, tile_col)

def pack_blocks(grads_dev, memory_dev, layer_ids, tile_row, tile_col):
    grad_tiles = take_tiles(grads_dev, layer_ids, tile_row, tile_col).astype(jnp.float32)
    memory_tiles = take_tiles(memory_dev, layer_ids, tile_row, tile_col).astype(jnp.float32)
    combined = grad_tiles + memory_tiles
    return combined.reshape(combined.shape[0], TILE * TILE)

def selected_mask(layer_ids, block_ids, layers, tile_count):
    columns = layer_ids * (tile_count * tile_count) + block_ids
    all_columns = jnp.arange(layers * tile_count * tile_count, dtype=jnp.int32)
    chosen = jnp.any(columns[:, None] == all_columns[None, :], axis=0)
    return chosen.reshape(layers, tile_count, 1, tile_count, 1)

def filter_memory(grads_dev, memory_dev, chosen):
    layers, model_width, _ = grads_dev.shape
    tile_count = model_width // TILE
    accumulated = grads_dev.astype(jnp.float32) + memory_dev.astype(jnp.float32)
    shaped = accumulated.reshape(layers, tile_count, TILE, tile_count, TILE)
    filtered = jnp.where(chosen, jnp.float32(0.0), shaped).reshape(layers, model_width, model_width)
    mixed = (1.0 - filter_rate) * memory_dev.astype(jnp.float32) + filter_rate * filtered
    return mixed.astype(jnp.bfloat16)

def adam_rows(summed, weights_sel, first_old, second_old):
    first_sel = beta_one * first_old + (1.0 - beta_one) * summed
    second_sel = beta_two * second_old + (1.0 - beta_two) * summed * summed
    update = first_sel / (jnp.sqrt(second_sel) + adam_eps) + weight_decay * weights_sel
    return (first_sel, second_sel, update)

def layer_squares(member, values):
    return lax.optimization_barrier(jnp.sum(member * lax.optimization_barrier(jnp.sum(values * values, axis=1))[:, None], axis=0))

def trust_rows(member, weight_total, update_total):
    trust_ratio = jnp.sqrt(weight_total / (update_total + norm_eps))
    return lax.optimization_barrier(jnp.sum(member * trust_ratio[None, :], axis=1))

def reference(grads, memory, block_ids, layer_ids, master, first_moment, second_moment):
    tile_count = D // TILE
    tile_row = block_ids // tile_count
    tile_col = block_ids % tile_count
    chosen = selected_mask(layer_ids, block_ids, LAYERS, tile_count)
    grads_view = grads.reshape(N_DP, LAYERS, D, D)
    memory_view = memory.reshape(N_DP, LAYERS, D, D)

    def per_device(running, arrays):
        grads_dev, memory_dev = arrays
        packed = pack_blocks(grads_dev, memory_dev, layer_ids, tile_row, tile_col)
        return (running + packed, filter_memory(grads_dev, memory_dev, chosen))
    summed, filtered_all = lax.scan(per_device, jnp.zeros((SEL, TILE * TILE), jnp.float32), (grads_view, memory_view))
    new_memory = filtered_all.reshape(N_DP * LAYERS, D, D)
    columns = layer_ids * BLOCKS_LAYER + block_ids
    weights_sel = jnp.take(master, columns, axis=0)
    first_old = jnp.take(first_moment, columns, axis=0)
    second_old = jnp.take(second_moment, columns, axis=0)
    first_sel, second_sel, update = adam_rows(summed, weights_sel, first_old, second_old)
    member = (layer_ids[:, None] == jnp.arange(LAYERS, dtype=jnp.int32)[None, :]).astype(jnp.float32)
    row_ratio = trust_rows(member, layer_squares(member, weights_sel), layer_squares(member, update))
    scaled = row_ratio[:, None] * update
    step_blocks = scaled.astype(jnp.bfloat16)
    master_new = master.at[columns].set(weights_sel - learn_rate * scaled)
    first_new = first_moment.at[columns].set(first_sel)
    second_new = second_moment.at[columns].set(second_sel)
    return (new_memory, master_new, first_new, second_new, step_blocks)
```

```python
import functools

import jax
import jax.numpy as jnp
from jax import lax
from jax.experimental import pallas as pl
from jax.experimental.pallas import tpu as pltpu
from jax.sharding import PartitionSpec as P

TILE = 128


filter_rate = 0.3
beta_one = 0.9
beta_two = 0.999
adam_eps = 1e-06
weight_decay = 0.01
learn_rate = 0.01
norm_eps = 1e-06


def take_tiles(source, layer_ids, tile_row, tile_col):

    def single(layer_id, row_tile, col_tile):
        return lax.dynamic_slice(
            source, (layer_id, row_tile * TILE, col_tile * TILE), (1, TILE, TILE)
        )[0]

    return jax.vmap(single)(layer_ids, tile_row, tile_col)


def pack_blocks(grads_dev, memory_dev, layer_ids, tile_row, tile_col):
    grad_tiles = take_tiles(grads_dev, layer_ids, tile_row, tile_col).astype(jnp.float32)
    memory_tiles = take_tiles(memory_dev, layer_ids, tile_row, tile_col).astype(jnp.float32)
    combined = grad_tiles + memory_tiles
    return combined.reshape(combined.shape[0], TILE * TILE)


def selected_mask(layer_ids, block_ids, layers, tile_count):
    columns = layer_ids * (tile_count * tile_count) + block_ids
    all_columns = jnp.arange(layers * tile_count * tile_count, dtype=jnp.int32)
    chosen = jnp.any(columns[:, None] == all_columns[None, :], axis=0)
    return chosen.reshape(layers, tile_count, 1, tile_count, 1)


def filter_memory(grads_dev, memory_dev, chosen):
    layers, model_width, _ = grads_dev.shape
    tile_count = model_width // TILE
    accumulated = grads_dev.astype(jnp.float32) + memory_dev.astype(jnp.float32)
    shaped = accumulated.reshape(layers, tile_count, TILE, tile_count, TILE)
    filtered = jnp.where(chosen, jnp.float32(0.0), shaped).reshape(layers, model_width, model_width)
    mixed = (1.0 - filter_rate) * memory_dev.astype(jnp.float32) + filter_rate * filtered
    return mixed.astype(jnp.bfloat16)


def adam_rows(summed, weights_sel, first_old, second_old):
    first_sel = beta_one * first_old + (1.0 - beta_one) * summed
    second_sel = beta_two * second_old + (1.0 - beta_two) * summed * summed
    update = first_sel / (jnp.sqrt(second_sel) + adam_eps) + weight_decay * weights_sel
    return (first_sel, second_sel, update)


def layer_squares(member, values):
    return jnp.sum(member * jnp.sum(values * values, axis=1)[:, None], axis=0)


def trust_rows(member, weight_total, update_total):
    trust_ratio = jnp.sqrt(weight_total / (update_total + norm_eps))
    return jnp.sum(member * trust_ratio[None, :], axis=1)


def on_device(grads, memory, block_ids, layer_ids, master, first_moment, second_moment):
    layers, model_width, _ = grads.shape
    tile_count = model_width // TILE
    tile_row = block_ids // tile_count
    tile_col = block_ids % tile_count
    columns = layer_ids * (tile_count * tile_count) + block_ids
    member = (layer_ids[:, None] == jnp.arange(layers, dtype=jnp.int32)[None, :]).astype(
        jnp.float32
    )
    weights_sel = jnp.take(master, columns, axis=0)
    first_old = jnp.take(first_moment, columns, axis=0)
    second_old = jnp.take(second_moment, columns, axis=0)
    packed = pack_blocks(grads, memory, layer_ids, tile_row, tile_col)
    summed = lax.psum_scatter(packed, "dp", scatter_dimension=1, tiled=True)
    first_sel, second_sel, update = adam_rows(summed, weights_sel, first_old, second_old)
    weight_total, update_total = lax.psum(
        (layer_squares(member, weights_sel), layer_squares(member, update)), "dp"
    )
    scaled = trust_rows(member, weight_total, update_total)[:, None] * update
    step_blocks = lax.all_gather(scaled.astype(jnp.bfloat16), "dp", axis=1, tiled=True)
    new_memory = filter_memory(
        grads, memory, selected_mask(layer_ids, block_ids, layers, tile_count)
    )
    master_new = master.at[columns].set(weights_sel - learn_rate * scaled)
    first_new = first_moment.at[columns].set(first_sel)
    second_new = second_moment.at[columns].set(second_sel)
    return (new_memory, master_new, first_new, second_new, step_blocks)


def xor_bit(bit, flip):
    return bit if flip == 0 else 1 - bit


def flip_bits(value, flip, size):
    out, weight = 0, 1
    while weight < size:
        bit = lax.rem(lax.div(value, weight), 2)
        out = out + weight * xor_bit(bit, (flip // weight) % 2)
        weight *= 2
    return out


def exchange_kernel(n, layers_smem, blocks_smem, grads_hbm, memory_hbm, master_hbm, first_hbm, second_hbm,
                    kept_ref, step_ref, old_ref, rows_ref,
                    grads_ref, memory_ref, packed, recv1, send2, recv2, send3, recv3,
                    stat_own, stat_in, stat_mid, stat_far, updates, others, state_ref, member_ref, rate_ref,
                    load_sem, old_sem, s1, r1, s2, r2, s3, r3, s4, r4, s5, r5, su, ru, sx, rx):
    depth = n // 8
    count = step_ref.shape[0]
    entries = step_ref.shape[1] // n
    pieces = entries // TILE
    lines = pieces * count
    layers, width, _ = grads_ref.shape
    tile_count = width // TILE
    layer_tiles = tile_count * tile_count
    plane_rows = 8 * pieces
    me = lax.axis_index("dp")
    core = lax.rem(me, 2)
    x = lax.rem(lax.div(me, 2), 2)
    y = lax.rem(lax.div(me, 4), 2)
    z = lax.div(me, 8)

    def layer_of(dz):
        return flip_bits(z, dz, depth)

    def plane(dq):
        return xor_bit(y, dq // 2) * 2 + xor_bit(x, dq % 2)

    def device(dz, dq, dc):
        return layer_of(dz) * 8 + plane(dq) * 2 + xor_bit(core, dc)

    def copy(src, dst, send, recv, peer):
        return pltpu.make_async_remote_copy(
            src_ref=src, dst_ref=dst, send_sem=send, recv_sem=recv,
            device_id=(peer,), device_id_type=pl.DeviceIdType.MESH)

    loads = []
    parts = load_sem.shape[1]
    step_rows = layers * width // parts
    for i in range(parts):
        layer, rows = i * step_rows // width, pl.ds(i * step_rows % width, step_rows)
        for s, (source, held) in enumerate(((grads_hbm, grads_ref), (memory_hbm, memory_ref))):
            loads.append(pltpu.make_async_copy(source.at[layer, rows], held.at[layer, rows], load_sem.at[s, i]))
            loads[-1].start()
    olds = []
    for s, source in enumerate((master_hbm, first_hbm, second_hbm)):
        olds.append(pltpu.make_async_copy(source, old_ref.at[s], old_sem.at[s]))
        olds[-1].start()

    barrier = pltpu.get_barrier_semaphore()
    peers = [device(0, i // 2, i % 2) for i in range(1, 8)] + [device(dz, 0, 1) for dz in range(1, depth)]
    for peer in peers:
        pl.semaphore_signal(barrier, inc=1, device_id=(peer,), device_id_type=pl.DeviceIdType.MESH)

    chosen_layer = [layers_smem[k] for k in range(count)]
    chosen_block = [blocks_smem[k] for k in range(count)]
    columns = [chosen_layer[k] * layer_tiles + chosen_block[k] for k in range(count)]
    shape = (layers * layer_tiles, TILE)
    tile_index = lax.broadcasted_iota(jnp.int32, shape, 0)
    rates = jnp.full(shape, filter_rate, jnp.float32)
    for k in range(count):
        rates = jnp.where(tile_index == columns[k], jnp.float32(0.0), rates)
    rate_ref[...] = rates
    order_index = lax.rem(lax.broadcasted_iota(jnp.int32, (lines, TILE), 0), count)
    line_layer = jnp.zeros((lines, TILE), jnp.int32)
    for k in range(count):
        line_layer = jnp.where(order_index == k, chosen_layer[k], line_layer)
    for l in range(layers):
        member_ref[l] = jnp.where(line_layer == l, jnp.float32(1.0), jnp.float32(0.0))
    stat_own[...] = jnp.zeros_like(stat_own)

    def filter_slabs(start, stop):
        @pl.loop(start, stop)
        def _(i):
            layer = lax.div(i, tile_count)
            rows = pl.ds(pl.multiple_of(lax.rem(i, tile_count) * TILE, TILE), TILE)
            for t in range(tile_count):
                lanes = slice(t * TILE, (t + 1) * TILE)
                rate = rate_ref[pl.ds(i * tile_count + t, 1), :]
                mixed = (rate + (1.0 - filter_rate)) * memory_ref[layer, rows, lanes].astype(jnp.float32)
                mixed = mixed + rate * grads_ref[layer, rows, lanes].astype(jnp.float32)
                kept_ref[layer, rows, lanes] = mixed.astype(kept_ref.dtype)

    slabs = layers * tile_count

    def half(dz, dq):
        return core if (dz == 0) == (dq == 0) else 1 - core

    for load in loads:
        load.wait()
    pl.semaphore_wait(barrier, len(peers))

    far = list(range(depth - 1, -1, -1))
    order = (3, 1, 2, 0)
    first_hop, second_hop, third_hop = {}, {}, {}
    for dz in far:
        at = layer_of(dz)
        for k in range(count):
            rows = pl.ds((lax.div(chosen_block[k], tile_count) * depth + at) * plane_rows, plane_rows)
            lanes = pl.ds(lax.rem(chosen_block[k], tile_count) * TILE, TILE)
            packed[dz, pl.ds(k, plane_rows, stride=count), :] = (
                grads_ref[chosen_layer[k], rows, lanes].astype(jnp.float32)
                + memory_ref[chosen_layer[k], rows, lanes].astype(jnp.float32))
        for dq in order:
            slot = dz * 4 + dq
            first_hop[slot] = copy(packed.at[dz, chunk_lines(plane(dq), 1 - half(dz, dq), lines)], recv1.at[slot],
                                   s1.at[slot], r1.at[slot], device(0, 0, 1))
            first_hop[slot].start()
    def own(dz, dq):
        return packed[dz, chunk_lines(plane(dq), half(dz, dq), lines), :]

    for dz in far:
        for dq in order[:3]:
            slot, place = dz * 4 + dq, dz * 3 + dq - 1
            first_hop[slot].wait_recv()
            send2[place] = own(dz, dq) + recv1[slot]
            second_hop[place] = copy(send2.at[place], recv2.at[place], s2.at[place], r2.at[place], device(0, dq, 1))
            second_hop[place].start()

    for old in olds:
        old.wait()
    for s in range(3):
        for k in range(count):
            line = old_ref[s, pl.ds(columns[k], 1), :]
            for j in range(pieces):
                state_ref[s, j * count + k:j * count + k + 1, :] = line[:, j * TILE:(j + 1) * TILE]
    weights = state_ref[0]
    for l in range(layers):
        stat_own[l:l + 1, :] = jnp.sum(member_ref[l] * (weights * weights), axis=0, keepdims=True)
    filter_slabs(0, slabs // 8)

    summed = None
    for dz in far:
        first_hop[dz * 4].wait_recv()
        for dq in range(3):
            second_hop[dz * 3 + dq].wait_recv()
        part = (own(dz, 0) + recv1[dz * 4]) + ((recv2[dz * 3] + recv2[dz * 3 + 1]) + recv2[dz * 3 + 2])
        if dz == 0:
            summed = part
        else:
            send3[dz - 1] = part
            third_hop[dz] = copy(send3.at[dz - 1], recv3.at[dz - 1], s3.at[dz - 1], r3.at[dz - 1], device(dz, 0, 1))
            third_hop[dz].start()
    filter_slabs(slabs // 8, slabs // 2)
    for dz in range(1, depth):
        third_hop[dz].wait_recv()
        summed = summed + recv3[dz - 1]

    first_sel = beta_one * state_ref[1] + (1.0 - beta_one) * summed
    second_sel = beta_two * state_ref[2] + (1.0 - beta_two) * summed * summed
    update = first_sel / (jnp.sqrt(second_sel) + adam_eps) + weight_decay * weights
    updates[0] = update
    ahead, across, near, away = {}, {}, [], []

    def lift(dz, dq, to_z, to_q, send, at):
        ahead[dz * 4 + dq] = copy(updates.at[at], updates.at[dz * 4 + dq], send, ru.at[dz * 4 + dq], device(to_z, to_q, 1))
        ahead[dz * 4 + dq].start()

    def cross(slot):
        across[slot] = copy(updates.at[slot], others.at[slot], sx.at[slot], rx.at[slot], device(0, 0, 1))
        across[slot].start()

    for dz in far[:-1]:
        lift(dz, 0, dz, 0, su.at[dz * 4], 0)
    for dq in order[:3]:
        lift(0, dq, 0, dq, su.at[dq], 0)
    for l in range(layers):
        stat_own[layers + l:layers + l + 1, :] = jnp.sum(member_ref[l] * (update * update), axis=0, keepdims=True)

    def spot(i):
        return plane(i // 2) * 2 + xor_bit(core, i % 2)

    for i in range(1, 8):
        near.append(copy(stat_own, stat_in.at[spot(0)], s4.at[i - 1], r4.at[i - 1], device(0, i // 2, i % 2)))
        near[-1].start()
    cross(0)
    rows_ref[1] = first_sel
    rows_ref[2] = second_sel
    stat_in[spot(0)] = stat_own[...]
    filter_slabs(slabs // 2, 3 * slabs // 4)
    ahead[4].wait_recv()
    for dq in order[:3]:
        lift(1, dq, 0, dq, su.at[4 + dq], 4)
    cross(4)
    for i in range(1, 8):
        copy(stat_own, stat_in.at[spot(i)], s4.at[i - 1], r4.at[i - 1], device(0, i // 2, i % 2)).wait_recv()
    total = stat_in[0]
    for i in range(1, 8):
        total = total + stat_in[i]
    stat_mid[...] = total
    for dz in range(1, depth):
        away.append(copy(stat_mid, stat_far.at[z], s5.at[dz - 1], r5.at[dz - 1], device(dz, 0, 1)))
        away[-1].start()
    stat_far[z] = total
    for dz in range(2, depth):
        ahead[dz * 4].wait_recv()
        for dq in order[:3]:
            lift(dz, dq, 0, dq, su.at[dz * 4 + dq], dz * 4)
        cross(dz * 4)
    for dq in order[:3]:
        ahead[dq].wait_recv()
        cross(dq)
    filter_slabs(3 * slabs // 4, slabs)
    for dz in range(1, depth):
        copy(stat_mid, stat_far.at[layer_of(dz)], s5.at[dz - 1], r5.at[dz - 1], device(dz, 0, 1)).wait_recv()
    total = stat_far[0]
    for at in range(1, depth):
        total = total + stat_far[at]
    sums = jnp.sum(total, axis=1, keepdims=True)
    factor = jnp.zeros_like(update)
    for l in range(layers):
        ratio = jnp.sqrt(sums[l:l + 1] / (sums[layers + l:layers + l + 1] + norm_eps))
        factor = factor + member_ref[l] * ratio
    rows_ref[0] = weights - learn_rate * (factor * update)

    def place(source, dz, dq, part):
        scaled = factor * source[dz * 4 + dq]
        owner = layer_of(dz) * 8 + plane(dq) * 2 + part
        for j in range(pieces):
            lanes = pl.ds(pl.multiple_of(owner * entries + j * TILE, TILE), TILE)
            step_ref[:, lanes] = scaled[j * count:(j + 1) * count].astype(step_ref.dtype)

    for dq in (0,) + order[:3]:
        place(updates, 0, dq, half(0, dq))
    for dz in range(1, depth):
        place(updates, dz, 0, half(dz, 0))
    for dz in range(1, depth):
        for dq in order[:3]:
            ahead[dz * 4 + dq].wait_recv()
            cross(dz * 4 + dq)
            place(updates, dz, dq, half(dz, dq))
    for slot in across:
        across[slot].wait_recv()
        place(others, slot // 4, slot % 4, 1 - half(slot // 4, slot % 4))
    started = near + away + [
        hop for hops in (first_hop, second_hop, third_hop, ahead, across) for hop in hops.values()]
    for hop in started:
        hop.wait_send()


def chunk_lines(plane_at, part, lines):
    return pl.ds(pl.multiple_of((plane_at * 2 + part) * lines, lines), lines)


def state_kernel(layers_smem, blocks_smem, kept_ref, step_ref, old_ref, rows_ref,
                 kept_out, master_out, first_out, second_out, step_out, new_ref, sem):
    count = layers_smem.shape[0]
    pieces = rows_ref.shape[1] // count
    layers, width, _ = kept_ref.shape
    layer_rows = (width // TILE) * (width // TILE)
    outs = [pltpu.make_async_copy(kept_ref.at[l], kept_out.at[l], sem.at[4 + l]) for l in range(layers)]
    outs.append(pltpu.make_async_copy(step_ref, step_out, sem.at[3]))
    for out in outs:
        out.start()
    for s, target in enumerate((master_out, first_out, second_out)):
        new_ref[s] = old_ref[s]
        for k in range(count):
            column = layers_smem[k] * layer_rows + blocks_smem[k]
            base = pl.ds(pl.multiple_of(lax.div(column, 8) * 8, 8), 8)
            hit = lax.broadcasted_iota(jnp.int32, (8, TILE), 0) == lax.rem(column, 8)
            for j in range(pieces):
                lanes = slice(j * TILE, (j + 1) * TILE)
                line = rows_ref[s, j * count + k:j * count + k + 1, :]
                new_ref[s, base, lanes] = jnp.where(hit, line, new_ref[s, base, lanes])
        outs.append(pltpu.make_async_copy(new_ref.at[s], target, sem.at[s]))
        outs[-1].start()
    for out in outs:
        out.wait()


def on_device_kernels(n, grads, memory, block_ids, layer_ids, master, first_moment, second_moment):
    layers, width, _ = grads.shape
    tile_count = width // TILE
    count = block_ids.shape[0]
    entries = master.shape[1]
    lines = entries // TILE * count
    depth = n // 8
    f32 = jnp.float32
    vmem, smem, hbm = (pl.BlockSpec(memory_space=m) for m in (pltpu.VMEM, pltpu.SMEM, pltpu.HBM))
    dma = pltpu.SemaphoreType.DMA
    stat_rows = -(-2 * layers // 8) * 8

    def chunks(*lead):
        return pltpu.VMEM(lead + (lines, TILE), f32)

    grads, memory, block_ids, layer_ids, master, first_moment, second_moment = (
        pltpu.with_memory_space_constraint(v, pltpu.HBM)
        for v in (grads, memory, block_ids, layer_ids, master, first_moment, second_moment))
    kept, step, old, rows = pl.pallas_call(
        functools.partial(exchange_kernel, n),
        out_shape=[pltpu.VMEM(memory.shape, jnp.bfloat16),
                   pltpu.VMEM((count, n * entries), jnp.bfloat16),
                   pltpu.VMEM((3,) + master.shape, f32),
                   chunks(3)],
        in_specs=[smem, smem] + [hbm] * 5,
        out_specs=[vmem] * 4,
        scratch_shapes=[
            pltpu.VMEM(grads.shape, jnp.bfloat16), pltpu.VMEM(memory.shape, jnp.bfloat16),
            pltpu.VMEM((depth, 8 * lines, TILE), f32),
            chunks(depth * 4), chunks(depth * 3), chunks(depth * 3), chunks(depth - 1), chunks(depth - 1),
            pltpu.VMEM((stat_rows, TILE), f32),
            pltpu.VMEM((8, stat_rows, TILE), f32),
            pltpu.VMEM((stat_rows, TILE), f32),
            pltpu.VMEM((depth, stat_rows, TILE), f32),
            chunks(depth * 4), chunks(depth * 4), chunks(3), chunks(layers),
            pltpu.VMEM((layers * tile_count * tile_count, TILE), f32),
            dma((2, 4 * layers)), dma((3,)),
            dma((depth * 4,)), dma((depth * 4,)), dma((depth * 3,)), dma((depth * 3,)), dma((depth - 1,)), dma((depth - 1,)),
            dma((7,)), dma((7,)), dma((depth - 1,)), dma((depth - 1,)),
            dma((depth * 4,)), dma((depth * 4,)), dma((depth * 4,)), dma((depth * 4,))],
        compiler_params=pltpu.CompilerParams(collective_id=0, has_side_effects=True, vmem_limit_bytes=40 * 2 ** 20),
        name="exchange",
    )(layer_ids, block_ids, grads, memory, master, first_moment, second_moment)
    like = jax.ShapeDtypeStruct(master.shape, f32)
    new_memory, master_new, first_new, second_new, step_blocks = pl.pallas_call(
        state_kernel,
        out_shape=[jax.ShapeDtypeStruct(memory.shape, jnp.bfloat16)] + [like] * 3
        + [jax.ShapeDtypeStruct(step.shape, jnp.bfloat16)],
        in_specs=[smem, smem] + [vmem] * 4,
        out_specs=[hbm] * 5,
        scratch_shapes=[pltpu.VMEM((3,) + master.shape, f32), dma((4 + layers,))],
        compiler_params=pltpu.CompilerParams(vmem_limit_bytes=16 * 2 ** 20),
        name="state",
    )(layer_ids, block_ids, kept, step, old, rows)
    return (new_memory, master_new, first_new, second_new, step_blocks)


def solution(mesh):
    n = mesh.shape["dp"]
    depth = n // 8

    def body(*args):
        entries, count = args[4].shape[1], args[2].shape[0]
        if n % 8 == 0 and depth > 1 and depth & (depth - 1) == 0 and entries % TILE == 0 and count % 16 == 0:
            return on_device_kernels(n, *args)
        return on_device(*args)

    in_specs = (
        P("dp", None, None),
        P("dp", None, None),
        P(),
        P(),
        P(None, "dp"),
        P(None, "dp"),
        P(None, "dp"),
    )
    out_specs = (P("dp", None, None), P(None, "dp"), P(None, "dp"), P(None, "dp"), P())
    return jax.shard_map(
        body, mesh=mesh, in_specs=in_specs, out_specs=out_specs, check_vma=False
    )
```

```python
import functools

import jax
import jax.numpy as jnp
from jax import lax
from jax.experimental import pallas as pl
from jax.experimental.pallas import tpu as pltpu
from jax.sharding import PartitionSpec as P

TILE = 128


filter_rate = 0.3
beta_one = 0.9
beta_two = 0.999
adam_eps = 1e-06
weight_decay = 0.01
learn_rate = 0.01
norm_eps = 1e-06


def take_tiles(source, layer_ids, tile_row, tile_col):

    def single(layer_id, row_tile, col_tile):
        return lax.dynamic_slice(
            source, (layer_id, row_tile * TILE, col_tile * TILE), (1, TILE, TILE)
        )[0]

    return jax.vmap(single)(layer_ids, tile_row, tile_col)


def pack_blocks(grads_dev, memory_dev, layer_ids, tile_row, tile_col):
    grad_tiles = take_tiles(grads_dev, layer_ids, tile_row, tile_col).astype(jnp.float32)
    memory_tiles = take_tiles(memory_dev, layer_ids, tile_row, tile_col).astype(jnp.float32)
    combined = grad_tiles + memory_tiles
    return combined.reshape(combined.shape[0], TILE * TILE)


def selected_mask(layer_ids, block_ids, layers, tile_count):
    columns = layer_ids * (tile_count * tile_count) + block_ids
    all_columns = jnp.arange(layers * tile_count * tile_count, dtype=jnp.int32)
    chosen = jnp.any(columns[:, None] == all_columns[None, :], axis=0)
    return chosen.reshape(layers, tile_count, 1, tile_count, 1)


def filter_memory(grads_dev, memory_dev, chosen):
    layers, model_width, _ = grads_dev.shape
    tile_count = model_width // TILE
    accumulated = grads_dev.astype(jnp.float32) + memory_dev.astype(jnp.float32)
    shaped = accumulated.reshape(layers, tile_count, TILE, tile_count, TILE)
    filtered = jnp.where(chosen, jnp.float32(0.0), shaped).reshape(layers, model_width, model_width)
    mixed = (1.0 - filter_rate) * memory_dev.astype(jnp.float32) + filter_rate * filtered
    return mixed.astype(jnp.bfloat16)


def adam_rows(summed, weights_sel, first_old, second_old):
    first_sel = beta_one * first_old + (1.0 - beta_one) * summed
    second_sel = beta_two * second_old + (1.0 - beta_two) * summed * summed
    update = first_sel / (jnp.sqrt(second_sel) + adam_eps) + weight_decay * weights_sel
    return (first_sel, second_sel, update)


def layer_squares(member, values):
    return jnp.sum(member * jnp.sum(values * values, axis=1)[:, None], axis=0)


def trust_rows(member, weight_total, update_total):
    trust_ratio = jnp.sqrt(weight_total / (update_total + norm_eps))
    return jnp.sum(member * trust_ratio[None, :], axis=1)


def on_device(grads, memory, block_ids, layer_ids, master, first_moment, second_moment):
    layers, model_width, _ = grads.shape
    tile_count = model_width // TILE
    tile_row = block_ids // tile_count
    tile_col = block_ids % tile_count
    columns = layer_ids * (tile_count * tile_count) + block_ids
    member = (layer_ids[:, None] == jnp.arange(layers, dtype=jnp.int32)[None, :]).astype(
        jnp.float32
    )
    weights_sel = jnp.take(master, columns, axis=0)
    first_old = jnp.take(first_moment, columns, axis=0)
    second_old = jnp.take(second_moment, columns, axis=0)
    packed = pack_blocks(grads, memory, layer_ids, tile_row, tile_col)
    summed = lax.psum_scatter(packed, "dp", scatter_dimension=1, tiled=True)
    first_sel, second_sel, update = adam_rows(summed, weights_sel, first_old, second_old)
    weight_total, update_total = lax.psum(
        (layer_squares(member, weights_sel), layer_squares(member, update)), "dp"
    )
    scaled = trust_rows(member, weight_total, update_total)[:, None] * update
    step_blocks = lax.all_gather(scaled.astype(jnp.bfloat16), "dp", axis=1, tiled=True)
    new_memory = filter_memory(
        grads, memory, selected_mask(layer_ids, block_ids, layers, tile_count)
    )
    master_new = master.at[columns].set(weights_sel - learn_rate * scaled)
    first_new = first_moment.at[columns].set(first_sel)
    second_new = second_moment.at[columns].set(second_sel)
    return (new_memory, master_new, first_new, second_new, step_blocks)


def xor_bit(bit, flip):
    return bit if flip == 0 else 1 - bit


def flip_bits(value, flip, size):
    out, weight = 0, 1
    while weight < size:
        bit = lax.rem(lax.div(value, weight), 2)
        out = out + weight * xor_bit(bit, (flip // weight) % 2)
        weight *= 2
    return out


def exchange_kernel(n, layers_hbm, blocks_hbm, grads_hbm, memory_hbm, master_hbm, first_hbm, second_hbm,
                    kept_ref, step_ref, old_ref, rows_ref,
                    layers_smem, blocks_smem, grads_ref, memory_ref, packed, recv1, send2, recv2, send3, recv3,
                    stat_own, stat_in, stat_mid, stat_far, updates, others, state_ref, member_ref, rate_ref,
                    id_sem, load_sem, old_sem, s1, r1, s2, r2, s3, r3, s4, r4, s5, r5, su, ru, sx, rx):
    depth = n // 8
    count = step_ref.shape[0]
    entries = step_ref.shape[1] // n
    pieces = entries // TILE
    lines = pieces * count
    layers, width, _ = grads_ref.shape
    tile_count = width // TILE
    layer_tiles = tile_count * tile_count
    plane_rows = 8 * pieces
    me = lax.axis_index("dp")
    core = lax.rem(me, 2)
    x = lax.rem(lax.div(me, 2), 2)
    y = lax.rem(lax.div(me, 4), 2)
    z = lax.div(me, 8)

    def layer_of(dz):
        return flip_bits(z, dz, depth)

    def plane(dq):
        return xor_bit(y, dq // 2) * 2 + xor_bit(x, dq % 2)

    def device(dz, dq, dc):
        return layer_of(dz) * 8 + plane(dq) * 2 + xor_bit(core, dc)

    def copy(src, dst, send, recv, peer):
        return pltpu.make_async_remote_copy(
            src_ref=src, dst_ref=dst, send_sem=send, recv_sem=recv,
            device_id=(peer,), device_id_type=pl.DeviceIdType.MESH)

    names = [pltpu.make_async_copy(layers_hbm, layers_smem, id_sem.at[0]),
             pltpu.make_async_copy(blocks_hbm, blocks_smem, id_sem.at[1])]
    for name in names:
        name.start()
    loads = []
    parts = load_sem.shape[1]
    step_rows = layers * width // parts
    for i in range(parts):
        layer, rows = i * step_rows // width, pl.ds(i * step_rows % width, step_rows)
        for s, (source, held) in enumerate(((grads_hbm, grads_ref), (memory_hbm, memory_ref))):
            loads.append(pltpu.make_async_copy(source.at[layer, rows], held.at[layer, rows], load_sem.at[s, i]))
            loads[-1].start()
    olds = []
    for s, source in enumerate((master_hbm, first_hbm, second_hbm)):
        olds.append(pltpu.make_async_copy(source, old_ref.at[s], old_sem.at[s]))
        olds[-1].start()

    barrier = pltpu.get_barrier_semaphore()
    peers = [device(0, i // 2, i % 2) for i in range(1, 8)] + [device(dz, 0, 0) for dz in range(1, depth)]
    for peer in peers:
        pl.semaphore_signal(barrier, inc=1, device_id=(peer,), device_id_type=pl.DeviceIdType.MESH)

    for name in names:
        name.wait()
    chosen_layer = [layers_smem[k] for k in range(count)]
    chosen_block = [blocks_smem[k] for k in range(count)]
    columns = [chosen_layer[k] * layer_tiles + chosen_block[k] for k in range(count)]
    shape = (layers * layer_tiles, TILE)
    tile_index = lax.broadcasted_iota(jnp.int32, shape, 0)
    rates = jnp.full(shape, filter_rate, jnp.float32)
    for k in range(count):
        rates = jnp.where(tile_index == columns[k], jnp.float32(0.0), rates)
    rate_ref[...] = rates
    order_index = lax.rem(lax.broadcasted_iota(jnp.int32, (lines, TILE), 0), count)
    line_layer = jnp.zeros((lines, TILE), jnp.int32)
    for k in range(count):
        line_layer = jnp.where(order_index == k, chosen_layer[k], line_layer)
    for l in range(layers):
        member_ref[l] = jnp.where(line_layer == l, jnp.float32(1.0), jnp.float32(0.0))
    stat_own[...] = jnp.zeros_like(stat_own)

    def filter_slabs(start, stop):
        @pl.loop(start, stop)
        def _(i):
            layer = lax.div(i, tile_count)
            rows = pl.ds(pl.multiple_of(lax.rem(i, tile_count) * TILE, TILE), TILE)
            for t in range(tile_count):
                lanes = slice(t * TILE, (t + 1) * TILE)
                rate = rate_ref[pl.ds(i * tile_count + t, 1), :]
                mixed = (rate + (1.0 - filter_rate)) * memory_ref[layer, rows, lanes].astype(jnp.float32)
                mixed = mixed + rate * grads_ref[layer, rows, lanes].astype(jnp.float32)
                kept_ref[layer, rows, lanes] = mixed.astype(kept_ref.dtype)

    slabs = layers * tile_count

    for load in loads:
        load.wait()
    pl.semaphore_wait(barrier, len(peers))

    far = list(range(depth - 1, -1, -1))
    order = (3, 1, 2, 0)
    first_hop, second_hop, third_hop = {}, {}, {}
    for dz in far:
        at = layer_of(dz)
        for k in range(count):
            rows = pl.ds((lax.div(chosen_block[k], tile_count) * depth + at) * plane_rows, plane_rows)
            lanes = pl.ds(lax.rem(chosen_block[k], tile_count) * TILE, TILE)
            packed[dz, pl.ds(k, plane_rows, stride=count), :] = (
                grads_ref[chosen_layer[k], rows, lanes].astype(jnp.float32)
                + memory_ref[chosen_layer[k], rows, lanes].astype(jnp.float32))
        for dq in order:
            slot = dz * 4 + dq
            first_hop[slot] = copy(packed.at[dz, chunk_lines(plane(dq), 1 - core, lines)], recv1.at[slot],
                                   s1.at[slot], r1.at[slot], device(0, 0, 1))
            first_hop[slot].start()
    def own(dz, dq):
        return packed[dz, chunk_lines(plane(dq), core, lines), :]

    for dz in far:
        for dq in order[:3]:
            slot, place = dz * 4 + dq, dz * 3 + dq - 1
            first_hop[slot].wait_recv()
            send2[place] = own(dz, dq) + recv1[slot]
            second_hop[place] = copy(send2.at[place], recv2.at[place], s2.at[place], r2.at[place], device(0, dq, 0))
            second_hop[place].start()

    for old in olds:
        old.wait()
    for s in range(3):
        for k in range(count):
            line = old_ref[s, pl.ds(columns[k], 1), :]
            for j in range(pieces):
                state_ref[s, j * count + k:j * count + k + 1, :] = line[:, j * TILE:(j + 1) * TILE]
    weights = state_ref[0]
    for l in range(layers):
        stat_own[l:l + 1, :] = jnp.sum(member_ref[l] * (weights * weights), axis=0, keepdims=True)
    filter_slabs(0, slabs // 2)

    summed = None
    for dz in far:
        first_hop[dz * 4].wait_recv()
        for dq in range(3):
            second_hop[dz * 3 + dq].wait_recv()
        part = (own(dz, 0) + recv1[dz * 4]) + ((recv2[dz * 3] + recv2[dz * 3 + 1]) + recv2[dz * 3 + 2])
        if dz == 0:
            summed = part
        else:
            send3[dz - 1] = part
            third_hop[dz] = copy(send3.at[dz - 1], recv3.at[dz - 1], s3.at[dz - 1], r3.at[dz - 1], device(dz, 0, 0))
            third_hop[dz].start()
    for dz in range(1, depth):
        third_hop[dz].wait_recv()
        summed = summed + recv3[dz - 1]

    first_sel = beta_one * state_ref[1] + (1.0 - beta_one) * summed
    second_sel = beta_two * state_ref[2] + (1.0 - beta_two) * summed * summed
    update = first_sel / (jnp.sqrt(second_sel) + adam_eps) + weight_decay * weights
    updates[0] = update
    ahead, across, near, away = {}, {}, [], []

    def lift(dz, dq, to_z, to_q, send, at):
        ahead[dz * 4 + dq] = copy(updates.at[at], updates.at[dz * 4 + dq], send, ru.at[dz * 4 + dq], device(to_z, to_q, 0))
        ahead[dz * 4 + dq].start()

    def cross(slot):
        across[slot] = copy(updates.at[slot], others.at[slot], sx.at[slot], rx.at[slot], device(0, 0, 1))
        across[slot].start()

    for dz in far[:-1]:
        lift(dz, 0, dz, 0, su.at[dz * 4], 0)
    for dq in order[:3]:
        lift(0, dq, 0, dq, su.at[dq], 0)
    for l in range(layers):
        stat_own[layers + l:layers + l + 1, :] = jnp.sum(member_ref[l] * (update * update), axis=0, keepdims=True)

    def spot(i):
        return plane(i // 2) * 2 + xor_bit(core, i % 2)

    for i in range(1, 8):
        near.append(copy(stat_own, stat_in.at[spot(0)], s4.at[i - 1], r4.at[i - 1], device(0, i // 2, i % 2)))
        near[-1].start()
    cross(0)
    rows_ref[1] = first_sel
    rows_ref[2] = second_sel
    stat_in[spot(0)] = stat_own[...]
    filter_slabs(slabs // 2, slabs)
    for hops in (first_hop, second_hop, third_hop):
        for hop in hops.values():
            hop.wait_send()
    ahead[4].wait_recv()
    for dq in order[:3]:
        lift(1, dq, 0, dq, su.at[4 + dq], 4)
    cross(4)
    for i in range(1, 8):
        copy(stat_own, stat_in.at[spot(i)], s4.at[i - 1], r4.at[i - 1], device(0, i // 2, i % 2)).wait_recv()
    total = stat_in[0]
    for i in range(1, 8):
        total = total + stat_in[i]
    stat_mid[...] = total
    for dz in range(1, depth):
        away.append(copy(stat_mid, stat_far.at[z], s5.at[dz - 1], r5.at[dz - 1], device(dz, 0, 0)))
        away[-1].start()
    stat_far[z] = total
    for dz in range(2, depth):
        ahead[dz * 4].wait_recv()
        for dq in order[:3]:
            lift(dz, dq, 0, dq, su.at[dz * 4 + dq], dz * 4)
        cross(dz * 4)
    for dq in order[:3]:
        ahead[dq].wait_recv()
        cross(dq)
    for dz in range(1, depth):
        copy(stat_mid, stat_far.at[layer_of(dz)], s5.at[dz - 1], r5.at[dz - 1], device(dz, 0, 0)).wait_recv()
    total = stat_far[0]
    for at in range(1, depth):
        total = total + stat_far[at]
    sums = jnp.sum(total, axis=1, keepdims=True)
    factor = jnp.zeros_like(update)
    for l in range(layers):
        ratio = jnp.sqrt(sums[l:l + 1] / (sums[layers + l:layers + l + 1] + norm_eps))
        factor = factor + member_ref[l] * ratio
    rows_ref[0] = weights - learn_rate * (factor * update)

    def place(source, dz, dq, part):
        scaled = factor * source[dz * 4 + dq]
        owner = layer_of(dz) * 8 + plane(dq) * 2 + part
        for j in range(pieces):
            lanes = pl.ds(pl.multiple_of(owner * entries + j * TILE, TILE), TILE)
            step_ref[:, lanes] = scaled[j * count:(j + 1) * count].astype(step_ref.dtype)

    def mine(dz, dq):
        place(updates, dz, dq, core)

    def theirs(dz, dq):
        across[dz * 4 + dq].wait_recv()
        place(others, dz, dq, 1 - core)

    for dz in range(depth):
        mine(dz, 0)
    for dq in order[:3]:
        mine(0, dq)
    for dq in (0,) + order[:3]:
        theirs(0, dq)
    for hop in near + away:
        hop.wait_send()
    for dz in range(1, depth):
        for dq in order[:3]:
            ahead[dz * 4 + dq].wait_recv()
            cross(dz * 4 + dq)
            mine(dz, dq)
        theirs(dz, 0)
        if dz > 1:
            for dq in order[:3]:
                theirs(dz - 1, dq)
    for hop in ahead.values():
        hop.wait_send()
    for dq in order[:3]:
        theirs(depth - 1, dq)
    for hop in across.values():
        hop.wait_send()


def chunk_lines(plane_at, part, lines):
    return pl.ds(pl.multiple_of((plane_at * 2 + part) * lines, lines), lines)


def state_kernel(layers_hbm, blocks_hbm, kept_ref, step_ref, old_ref, rows_ref,
                 kept_out, master_out, first_out, second_out, step_out,
                 layers_smem, blocks_smem, new_ref, sem):
    count = layers_smem.shape[0]
    names = [pltpu.make_async_copy(layers_hbm, layers_smem, sem.at[0]),
             pltpu.make_async_copy(blocks_hbm, blocks_smem, sem.at[1])]
    for name in names:
        name.start()
    pieces = rows_ref.shape[1] // count
    layers, width, _ = kept_ref.shape
    layer_rows = (width // TILE) * (width // TILE)
    outs = [pltpu.make_async_copy(kept_ref.at[l], kept_out.at[l], sem.at[6 + l]) for l in range(layers)]
    outs.append(pltpu.make_async_copy(step_ref, step_out, sem.at[5]))
    for out in outs:
        out.start()
    for name in names:
        name.wait()
    for s, target in enumerate((master_out, first_out, second_out)):
        new_ref[s] = old_ref[s]
        for k in range(count):
            column = layers_smem[k] * layer_rows + blocks_smem[k]
            base = pl.ds(pl.multiple_of(lax.div(column, 8) * 8, 8), 8)
            hit = lax.broadcasted_iota(jnp.int32, (8, TILE), 0) == lax.rem(column, 8)
            for j in range(pieces):
                lanes = slice(j * TILE, (j + 1) * TILE)
                line = rows_ref[s, j * count + k:j * count + k + 1, :]
                new_ref[s, base, lanes] = jnp.where(hit, line, new_ref[s, base, lanes])
        outs.append(pltpu.make_async_copy(new_ref.at[s], target, sem.at[2 + s]))
        outs[-1].start()
    for out in outs:
        out.wait()


def on_device_kernels(n, grads, memory, block_ids, layer_ids, master, first_moment, second_moment):
    layers, width, _ = grads.shape
    tile_count = width // TILE
    count = block_ids.shape[0]
    entries = master.shape[1]
    lines = entries // TILE * count
    depth = n // 8
    f32 = jnp.float32
    vmem, hbm = (pl.BlockSpec(memory_space=m) for m in (pltpu.VMEM, pltpu.HBM))
    dma = pltpu.SemaphoreType.DMA
    stat_rows = -(-2 * layers // 8) * 8

    def chunks(*lead):
        return pltpu.VMEM(lead + (lines, TILE), f32)

    grads, memory, block_ids, layer_ids, master, first_moment, second_moment = (
        pltpu.with_memory_space_constraint(v, pltpu.HBM)
        for v in (grads, memory, block_ids, layer_ids, master, first_moment, second_moment))
    kept, step, old, rows = pl.pallas_call(
        functools.partial(exchange_kernel, n),
        out_shape=[pltpu.VMEM(memory.shape, jnp.bfloat16),
                   pltpu.VMEM((count, n * entries), jnp.bfloat16),
                   pltpu.VMEM((3,) + master.shape, f32),
                   chunks(3)],
        in_specs=[hbm] * 7,
        out_specs=[vmem] * 4,
        scratch_shapes=[
            pltpu.SMEM((count,), jnp.int32), pltpu.SMEM((count,), jnp.int32),
            pltpu.VMEM(grads.shape, jnp.bfloat16), pltpu.VMEM(memory.shape, jnp.bfloat16),
            pltpu.VMEM((depth, 8 * lines, TILE), f32),
            chunks(depth * 4), chunks(depth * 3), chunks(depth * 3), chunks(depth - 1), chunks(depth - 1),
            pltpu.VMEM((stat_rows, TILE), f32),
            pltpu.VMEM((8, stat_rows, TILE), f32),
            pltpu.VMEM((stat_rows, TILE), f32),
            pltpu.VMEM((depth, stat_rows, TILE), f32),
            chunks(depth * 4), chunks(depth * 4), chunks(3), chunks(layers),
            pltpu.VMEM((layers * tile_count * tile_count, TILE), f32),
            dma((2,)), dma((2, 4 * layers)), dma((3,)),
            dma((depth * 4,)), dma((depth * 4,)), dma((depth * 3,)), dma((depth * 3,)), dma((depth - 1,)), dma((depth - 1,)),
            dma((7,)), dma((7,)), dma((depth - 1,)), dma((depth - 1,)),
            dma((depth * 4,)), dma((depth * 4,)), dma((depth * 4,)), dma((depth * 4,))],
        compiler_params=pltpu.CompilerParams(collective_id=0, has_side_effects=True, vmem_limit_bytes=40 * 2 ** 20),
        name="exchange",
    )(layer_ids, block_ids, grads, memory, master, first_moment, second_moment)
    like = jax.ShapeDtypeStruct(master.shape, f32)
    new_memory, master_new, first_new, second_new, step_blocks = pl.pallas_call(
        state_kernel,
        out_shape=[jax.ShapeDtypeStruct(memory.shape, jnp.bfloat16)] + [like] * 3
        + [jax.ShapeDtypeStruct(step.shape, jnp.bfloat16)],
        in_specs=[hbm, hbm] + [vmem] * 4,
        out_specs=[hbm] * 5,
        scratch_shapes=[pltpu.SMEM((count,), jnp.int32), pltpu.SMEM((count,), jnp.int32),
                        pltpu.VMEM((3,) + master.shape, f32), dma((6 + layers,))],
        compiler_params=pltpu.CompilerParams(vmem_limit_bytes=16 * 2 ** 20),
        name="state",
    )(layer_ids, block_ids, kept, step, old, rows)
    return (new_memory, master_new, first_new, second_new, step_blocks)


def solution(mesh):
    n = mesh.shape["dp"]
    depth = n // 8

    def body(*args):
        entries, count = args[4].shape[1], args[2].shape[0]
        if n % 8 == 0 and depth > 1 and depth & (depth - 1) == 0 and entries % TILE == 0 and count % 16 == 0:
            return on_device_kernels(n, *args)
        return on_device(*args)

    in_specs = (
        P("dp", None, None),
        P("dp", None, None),
        P(),
        P(),
        P(None, "dp"),
        P(None, "dp"),
        P(None, "dp"),
    )
    out_specs = (P("dp", None, None), P(None, "dp"), P(None, "dp"), P(None, "dp"), P())
    return jax.shard_map(
        body, mesh=mesh, in_specs=in_specs, out_specs=out_specs, check_vma=False
    )
```

```python
import functools

import jax
import jax.numpy as jnp
from jax import lax
from jax.experimental import pallas as pl
from jax.experimental.pallas import tpu as pltpu
from jax.sharding import PartitionSpec as P

TILE = 128


filter_rate = 0.3
beta_one = 0.9
beta_two = 0.999
adam_eps = 1e-06
weight_decay = 0.01
learn_rate = 0.01
norm_eps = 1e-06


def take_tiles(source, layer_ids, tile_row, tile_col):

    def single(layer_id, row_tile, col_tile):
        return lax.dynamic_slice(
            source, (layer_id, row_tile * TILE, col_tile * TILE), (1, TILE, TILE)
        )[0]

    return jax.vmap(single)(layer_ids, tile_row, tile_col)


def pack_blocks(grads_dev, memory_dev, layer_ids, tile_row, tile_col):
    grad_tiles = take_tiles(grads_dev, layer_ids, tile_row, tile_col).astype(jnp.float32)
    memory_tiles = take_tiles(memory_dev, layer_ids, tile_row, tile_col).astype(jnp.float32)
    combined = grad_tiles + memory_tiles
    return combined.reshape(combined.shape[0], TILE * TILE)


def selected_mask(layer_ids, block_ids, layers, tile_count):
    columns = layer_ids * (tile_count * tile_count) + block_ids
    all_columns = jnp.arange(layers * tile_count * tile_count, dtype=jnp.int32)
    chosen = jnp.any(columns[:, None] == all_columns[None, :], axis=0)
    return chosen.reshape(layers, tile_count, 1, tile_count, 1)


def filter_memory(grads_dev, memory_dev, chosen):
    layers, model_width, _ = grads_dev.shape
    tile_count = model_width // TILE
    accumulated = grads_dev.astype(jnp.float32) + memory_dev.astype(jnp.float32)
    shaped = accumulated.reshape(layers, tile_count, TILE, tile_count, TILE)
    filtered = jnp.where(chosen, jnp.float32(0.0), shaped).reshape(layers, model_width, model_width)
    mixed = (1.0 - filter_rate) * memory_dev.astype(jnp.float32) + filter_rate * filtered
    return mixed.astype(jnp.bfloat16)


def adam_rows(summed, weights_sel, first_old, second_old):
    first_sel = beta_one * first_old + (1.0 - beta_one) * summed
    second_sel = beta_two * second_old + (1.0 - beta_two) * summed * summed
    update = first_sel / (jnp.sqrt(second_sel) + adam_eps) + weight_decay * weights_sel
    return (first_sel, second_sel, update)


def layer_squares(member, values):
    return jnp.sum(member * jnp.sum(values * values, axis=1)[:, None], axis=0)


def trust_rows(member, weight_total, update_total):
    trust_ratio = jnp.sqrt(weight_total / (update_total + norm_eps))
    return jnp.sum(member * trust_ratio[None, :], axis=1)


def on_device(grads, memory, block_ids, layer_ids, master, first_moment, second_moment):
    layers, model_width, _ = grads.shape
    tile_count = model_width // TILE
    tile_row = block_ids // tile_count
    tile_col = block_ids % tile_count
    columns = layer_ids * (tile_count * tile_count) + block_ids
    member = (layer_ids[:, None] == jnp.arange(layers, dtype=jnp.int32)[None, :]).astype(
        jnp.float32
    )
    weights_sel = jnp.take(master, columns, axis=0)
    first_old = jnp.take(first_moment, columns, axis=0)
    second_old = jnp.take(second_moment, columns, axis=0)
    packed = pack_blocks(grads, memory, layer_ids, tile_row, tile_col)
    summed = lax.psum_scatter(packed, "dp", scatter_dimension=1, tiled=True)
    first_sel, second_sel, update = adam_rows(summed, weights_sel, first_old, second_old)
    weight_total, update_total = lax.psum(
        (layer_squares(member, weights_sel), layer_squares(member, update)), "dp"
    )
    scaled = trust_rows(member, weight_total, update_total)[:, None] * update
    step_blocks = lax.all_gather(scaled.astype(jnp.bfloat16), "dp", axis=1, tiled=True)
    new_memory = filter_memory(
        grads, memory, selected_mask(layer_ids, block_ids, layers, tile_count)
    )
    master_new = master.at[columns].set(weights_sel - learn_rate * scaled)
    first_new = first_moment.at[columns].set(first_sel)
    second_new = second_moment.at[columns].set(second_sel)
    return (new_memory, master_new, first_new, second_new, step_blocks)


def xor_bit(bit, flip):
    return bit if flip == 0 else 1 - bit


def flip_bits(value, flip, size):
    out, weight = 0, 1
    while weight < size:
        bit = lax.rem(lax.div(value, weight), 2)
        out = out + weight * xor_bit(bit, (flip // weight) % 2)
        weight *= 2
    return out


def exchange_kernel(n, layers_hbm, blocks_hbm, grads_hbm, memory_hbm, master_hbm, first_hbm, second_hbm,
                    kept_ref, step_ref, old_ref, rows_ref,
                    layers_smem, blocks_smem, grads_ref, memory_ref, packed, recv1, send2, recv2, send3, recv3,
                    stat_own, stat_in, stat_mid, stat_far, updates, others, state_ref, member_ref, rate_ref,
                    id_sem, load_sem, old_sem, s1, r1, s2, r2, s3, r3, s4, r4, s5, r5, su, ru, sx, rx):
    depth = n // 8
    count = step_ref.shape[0]
    entries = step_ref.shape[1] // n
    pieces = entries // TILE
    lines = pieces * count
    layers, width, _ = grads_ref.shape
    tile_count = width // TILE
    layer_tiles = tile_count * tile_count
    plane_rows = 8 * pieces
    me = lax.axis_index("dp")
    core = lax.rem(me, 2)
    x = lax.rem(lax.div(me, 2), 2)
    y = lax.rem(lax.div(me, 4), 2)
    z = lax.div(me, 8)

    def layer_of(dz):
        return flip_bits(z, dz, depth)

    def plane(dq):
        return xor_bit(y, dq // 2) * 2 + xor_bit(x, dq % 2)

    def device(dz, dq, dc):
        return layer_of(dz) * 8 + plane(dq) * 2 + xor_bit(core, dc)

    def copy(src, dst, send, recv, peer):
        return pltpu.make_async_remote_copy(
            src_ref=src, dst_ref=dst, send_sem=send, recv_sem=recv,
            device_id=(peer,), device_id_type=pl.DeviceIdType.MESH)

    names = [pltpu.make_async_copy(layers_hbm, layers_smem, id_sem.at[0]),
             pltpu.make_async_copy(blocks_hbm, blocks_smem, id_sem.at[1])]
    for name in names:
        name.start()
    loads = []
    parts = load_sem.shape[1]
    step_rows = layers * width // parts
    for i in range(parts):
        layer, rows = i * step_rows // width, pl.ds(i * step_rows % width, step_rows)
        for s, (source, held) in enumerate(((grads_hbm, grads_ref), (memory_hbm, memory_ref))):
            loads.append(pltpu.make_async_copy(source.at[layer, rows], held.at[layer, rows], load_sem.at[s, i]))
            loads[-1].start()

    barrier = pltpu.get_barrier_semaphore()
    peers = [device(0, i // 2, i % 2) for i in range(1, 8)] + [device(dz, 0, 0) for dz in range(1, depth)]
    for peer in peers:
        pl.semaphore_signal(barrier, inc=1, device_id=(peer,), device_id_type=pl.DeviceIdType.MESH)

    for name in names:
        name.wait()
    chosen_layer = [layers_smem[k] for k in range(count)]
    chosen_block = [blocks_smem[k] for k in range(count)]
    columns = [chosen_layer[k] * layer_tiles + chosen_block[k] for k in range(count)]
    shape = (layers * layer_tiles, TILE)
    tile_index = lax.broadcasted_iota(jnp.int32, shape, 0)
    rates = jnp.full(shape, filter_rate, jnp.float32)
    for k in range(count):
        rates = jnp.where(tile_index == columns[k], jnp.float32(0.0), rates)
    rate_ref[...] = rates
    order_index = lax.rem(lax.broadcasted_iota(jnp.int32, (lines, TILE), 0), count)
    line_layer = jnp.zeros((lines, TILE), jnp.int32)
    for k in range(count):
        line_layer = jnp.where(order_index == k, chosen_layer[k], line_layer)
    for l in range(layers):
        member_ref[l] = jnp.where(line_layer == l, jnp.float32(1.0), jnp.float32(0.0))
    stat_own[...] = jnp.zeros_like(stat_own)

    def filter_slabs(start, stop):
        @pl.loop(start, stop)
        def _(i):
            layer = lax.div(i, tile_count)
            rows = pl.ds(pl.multiple_of(lax.rem(i, tile_count) * TILE, TILE), TILE)
            for t in range(tile_count):
                lanes = slice(t * TILE, (t + 1) * TILE)
                rate = rate_ref[pl.ds(i * tile_count + t, 1), :]
                mixed = (rate + (1.0 - filter_rate)) * memory_ref[layer, rows, lanes].astype(jnp.float32)
                mixed = mixed + rate * grads_ref[layer, rows, lanes].astype(jnp.float32)
                kept_ref[layer, rows, lanes] = mixed.astype(kept_ref.dtype)

    slabs = layers * tile_count

    for load in loads:
        load.wait()
    pl.semaphore_wait(barrier, len(peers))

    far = list(range(depth - 1, -1, -1))
    order = (3, 1, 2, 0)
    first_hop, second_hop, third_hop = {}, {}, {}
    for dz in far:
        at = layer_of(dz)
        for k in range(count):
            rows = pl.ds((lax.div(chosen_block[k], tile_count) * depth + at) * plane_rows, plane_rows)
            lanes = pl.ds(lax.rem(chosen_block[k], tile_count) * TILE, TILE)
            packed[dz, pl.ds(k, plane_rows, stride=count), :] = (
                grads_ref[chosen_layer[k], rows, lanes].astype(jnp.float32)
                + memory_ref[chosen_layer[k], rows, lanes].astype(jnp.float32))
        for dq in order:
            slot = dz * 4 + dq
            first_hop[slot] = copy(packed.at[dz, chunk_lines(plane(dq), 1 - core, lines)], recv1.at[slot],
                                   s1.at[slot], r1.at[slot], device(0, 0, 1))
            first_hop[slot].start()
    olds = []
    for s, source in enumerate((master_hbm, first_hbm, second_hbm)):
        olds.append(pltpu.make_async_copy(source, old_ref.at[s], old_sem.at[s]))
        olds[-1].start()
    def own(dz, dq):
        return packed[dz, chunk_lines(plane(dq), core, lines), :]

    for dz in far:
        for dq in order[:3]:
            slot, place = dz * 4 + dq, dz * 3 + dq - 1
            first_hop[slot].wait_recv()
            send2[place] = own(dz, dq) + recv1[slot]
            second_hop[place] = copy(send2.at[place], recv2.at[place], s2.at[place], r2.at[place], device(0, dq, 0))
            second_hop[place].start()

    for old in olds:
        old.wait()
    for s in range(3):
        for k in range(count):
            line = old_ref[s, pl.ds(columns[k], 1), :]
            for j in range(pieces):
                state_ref[s, j * count + k:j * count + k + 1, :] = line[:, j * TILE:(j + 1) * TILE]
    weights = state_ref[0]
    for l in range(layers):
        stat_own[l:l + 1, :] = jnp.sum(member_ref[l] * (weights * weights), axis=0, keepdims=True)
    filter_slabs(0, slabs // 2)

    summed = None
    for dz in far:
        first_hop[dz * 4].wait_recv()
        for dq in range(3):
            second_hop[dz * 3 + dq].wait_recv()
        part = (own(dz, 0) + recv1[dz * 4]) + ((recv2[dz * 3] + recv2[dz * 3 + 1]) + recv2[dz * 3 + 2])
        if dz == 0:
            summed = part
        else:
            send3[dz - 1] = part
            third_hop[dz] = copy(send3.at[dz - 1], recv3.at[dz - 1], s3.at[dz - 1], r3.at[dz - 1], device(dz, 0, 0))
            third_hop[dz].start()
    for dz in range(1, depth):
        third_hop[dz].wait_recv()
        summed = summed + recv3[dz - 1]

    first_sel = beta_one * state_ref[1] + (1.0 - beta_one) * summed
    second_sel = beta_two * state_ref[2] + (1.0 - beta_two) * summed * summed
    update = first_sel / (jnp.sqrt(second_sel) + adam_eps) + weight_decay * weights
    updates[0] = update
    ahead, across, near, away = {}, {}, [], []

    def lift(dz, dq, to_z, to_q, send, at):
        ahead[dz * 4 + dq] = copy(updates.at[at], updates.at[dz * 4 + dq], send, ru.at[dz * 4 + dq], device(to_z, to_q, 0))
        ahead[dz * 4 + dq].start()

    def cross(slot):
        across[slot] = copy(updates.at[slot], others.at[slot], sx.at[slot], rx.at[slot], device(0, 0, 1))
        across[slot].start()

    for dz in far[:-1]:
        lift(dz, 0, dz, 0, su.at[dz * 4], 0)
    for dq in order[:3]:
        lift(0, dq, 0, dq, su.at[dq], 0)
    for l in range(layers):
        stat_own[layers + l:layers + l + 1, :] = jnp.sum(member_ref[l] * (update * update), axis=0, keepdims=True)

    def spot(i):
        return plane(i // 2) * 2 + xor_bit(core, i % 2)

    for i in range(1, 8):
        near.append(copy(stat_own, stat_in.at[spot(0)], s4.at[i - 1], r4.at[i - 1], device(0, i // 2, i % 2)))
        near[-1].start()
    cross(0)
    rows_ref[1] = first_sel
    rows_ref[2] = second_sel
    stat_in[spot(0)] = stat_own[...]
    filter_slabs(slabs // 2, slabs)
    for hops in (first_hop, second_hop, third_hop):
        for hop in hops.values():
            hop.wait_send()
    ahead[4].wait_recv()
    for dq in order[:3]:
        lift(1, dq, 0, dq, su.at[4 + dq], 4)
    cross(4)
    for i in range(1, 8):
        copy(stat_own, stat_in.at[spot(i)], s4.at[i - 1], r4.at[i - 1], device(0, i // 2, i % 2)).wait_recv()
    total = stat_in[0]
    for i in range(1, 8):
        total = total + stat_in[i]
    stat_mid[...] = total
    for dz in range(1, depth):
        away.append(copy(stat_mid, stat_far.at[z], s5.at[dz - 1], r5.at[dz - 1], device(dz, 0, 0)))
        away[-1].start()
    stat_far[z] = total
    for dz in range(2, depth):
        ahead[dz * 4].wait_recv()
        for dq in order[:3]:
            lift(dz, dq, 0, dq, su.at[dz * 4 + dq], dz * 4)
        cross(dz * 4)
    for dq in order[:3]:
        ahead[dq].wait_recv()
        cross(dq)
    for dz in range(1, depth):
        copy(stat_mid, stat_far.at[layer_of(dz)], s5.at[dz - 1], r5.at[dz - 1], device(dz, 0, 0)).wait_recv()
    total = stat_far[0]
    for at in range(1, depth):
        total = total + stat_far[at]
    sums = jnp.sum(total, axis=1, keepdims=True)
    factor = jnp.zeros_like(update)
    for l in range(layers):
        ratio = jnp.sqrt(sums[l:l + 1] / (sums[layers + l:layers + l + 1] + norm_eps))
        factor = factor + member_ref[l] * ratio
    rows_ref[0] = weights - learn_rate * (factor * update)

    def place(source, dz, dq, part):
        scaled = factor * source[dz * 4 + dq]
        owner = layer_of(dz) * 8 + plane(dq) * 2 + part
        for j in range(pieces):
            lanes = pl.ds(pl.multiple_of(owner * entries + j * TILE, TILE), TILE)
            step_ref[:, lanes] = scaled[j * count:(j + 1) * count].astype(step_ref.dtype)

    def mine(dz, dq):
        place(updates, dz, dq, core)

    def theirs(dz, dq):
        across[dz * 4 + dq].wait_recv()
        place(others, dz, dq, 1 - core)

    for dz in range(depth):
        mine(dz, 0)
    for dq in order[:3]:
        mine(0, dq)
    for dq in (0,) + order[:3]:
        theirs(0, dq)
    for hop in near + away:
        hop.wait_send()
    for dz in range(1, depth):
        for dq in order[:3]:
            ahead[dz * 4 + dq].wait_recv()
            cross(dz * 4 + dq)
            mine(dz, dq)
        theirs(dz, 0)
        if dz > 1:
            for dq in order[:3]:
                theirs(dz - 1, dq)
    for hop in ahead.values():
        hop.wait_send()
    for dq in order[:3]:
        theirs(depth - 1, dq)
    for hop in across.values():
        hop.wait_send()


def chunk_lines(plane_at, part, lines):
    return pl.ds(pl.multiple_of((plane_at * 2 + part) * lines, lines), lines)


def state_kernel(layers_hbm, blocks_hbm, kept_ref, step_ref, old_ref, rows_ref,
                 kept_out, master_out, first_out, second_out, step_out,
                 layers_smem, blocks_smem, new_ref, sem):
    count = layers_smem.shape[0]
    names = [pltpu.make_async_copy(layers_hbm, layers_smem, sem.at[0]),
             pltpu.make_async_copy(blocks_hbm, blocks_smem, sem.at[1])]
    for name in names:
        name.start()
    pieces = rows_ref.shape[1] // count
    layers, width, _ = kept_ref.shape
    layer_rows = (width // TILE) * (width // TILE)
    outs = [pltpu.make_async_copy(kept_ref.at[l], kept_out.at[l], sem.at[6 + l]) for l in range(layers)]
    outs.append(pltpu.make_async_copy(step_ref, step_out, sem.at[5]))
    for out in outs:
        out.start()
    for name in names:
        name.wait()
    for s, target in enumerate((master_out, first_out, second_out)):
        new_ref[s] = old_ref[s]
        for k in range(count):
            column = layers_smem[k] * layer_rows + blocks_smem[k]
            base = pl.ds(pl.multiple_of(lax.div(column, 8) * 8, 8), 8)
            hit = lax.broadcasted_iota(jnp.int32, (8, TILE), 0) == lax.rem(column, 8)
            for j in range(pieces):
                lanes = slice(j * TILE, (j + 1) * TILE)
                line = rows_ref[s, j * count + k:j * count + k + 1, :]
                new_ref[s, base, lanes] = jnp.where(hit, line, new_ref[s, base, lanes])
        outs.append(pltpu.make_async_copy(new_ref.at[s], target, sem.at[2 + s]))
        outs[-1].start()
    for out in outs:
        out.wait()


def on_device_kernels(n, grads, memory, block_ids, layer_ids, master, first_moment, second_moment):
    layers, width, _ = grads.shape
    tile_count = width // TILE
    count = block_ids.shape[0]
    entries = master.shape[1]
    lines = entries // TILE * count
    depth = n // 8
    f32 = jnp.float32
    vmem, hbm = (pl.BlockSpec(memory_space=m) for m in (pltpu.VMEM, pltpu.HBM))
    dma = pltpu.SemaphoreType.DMA
    stat_rows = -(-2 * layers // 8) * 8

    def chunks(*lead):
        return pltpu.VMEM(lead + (lines, TILE), f32)

    grads, memory, block_ids, layer_ids, master, first_moment, second_moment = (
        pltpu.with_memory_space_constraint(v, pltpu.HBM)
        for v in (grads, memory, block_ids, layer_ids, master, first_moment, second_moment))
    kept, step, old, rows = pl.pallas_call(
        functools.partial(exchange_kernel, n),
        out_shape=[pltpu.VMEM(memory.shape, jnp.bfloat16),
                   pltpu.VMEM((count, n * entries), jnp.bfloat16),
                   pltpu.VMEM((3,) + master.shape, f32),
                   chunks(3)],
        in_specs=[hbm] * 7,
        out_specs=[vmem] * 4,
        scratch_shapes=[
            pltpu.SMEM((count,), jnp.int32), pltpu.SMEM((count,), jnp.int32),
            pltpu.VMEM(grads.shape, jnp.bfloat16), pltpu.VMEM(memory.shape, jnp.bfloat16),
            pltpu.VMEM((depth, 8 * lines, TILE), f32),
            chunks(depth * 4), chunks(depth * 3), chunks(depth * 3), chunks(depth - 1), chunks(depth - 1),
            pltpu.VMEM((stat_rows, TILE), f32),
            pltpu.VMEM((8, stat_rows, TILE), f32),
            pltpu.VMEM((stat_rows, TILE), f32),
            pltpu.VMEM((depth, stat_rows, TILE), f32),
            chunks(depth * 4), chunks(depth * 4), chunks(3), chunks(layers),
            pltpu.VMEM((layers * tile_count * tile_count, TILE), f32),
            dma((2,)), dma((2, 4 * layers)), dma((3,)),
            dma((depth * 4,)), dma((depth * 4,)), dma((depth * 3,)), dma((depth * 3,)), dma((depth - 1,)), dma((depth - 1,)),
            dma((7,)), dma((7,)), dma((depth - 1,)), dma((depth - 1,)),
            dma((depth * 4,)), dma((depth * 4,)), dma((depth * 4,)), dma((depth * 4,))],
        compiler_params=pltpu.CompilerParams(collective_id=0, has_side_effects=True, vmem_limit_bytes=40 * 2 ** 20),
        name="exchange",
    )(layer_ids, block_ids, grads, memory, master, first_moment, second_moment)
    like = jax.ShapeDtypeStruct(master.shape, f32)
    new_memory, master_new, first_new, second_new, step_blocks = pl.pallas_call(
        state_kernel,
        out_shape=[jax.ShapeDtypeStruct(memory.shape, jnp.bfloat16)] + [like] * 3
        + [jax.ShapeDtypeStruct(step.shape, jnp.bfloat16)],
        in_specs=[hbm, hbm] + [vmem] * 4,
        out_specs=[hbm] * 5,
        scratch_shapes=[pltpu.SMEM((count,), jnp.int32), pltpu.SMEM((count,), jnp.int32),
                        pltpu.VMEM((3,) + master.shape, f32), dma((6 + layers,))],
        compiler_params=pltpu.CompilerParams(vmem_limit_bytes=16 * 2 ** 20),
        name="state",
    )(layer_ids, block_ids, kept, step, old, rows)
    return (new_memory, master_new, first_new, second_new, step_blocks)


def solution(mesh):
    n = mesh.shape["dp"]
    depth = n // 8

    def body(*args):
        entries, count = args[4].shape[1], args[2].shape[0]
        if n % 8 == 0 and depth > 1 and depth & (depth - 1) == 0 and entries % TILE == 0 and count % 16 == 0:
            return on_device_kernels(n, *args)
        return on_device(*args)

    in_specs = (
        P("dp", None, None),
        P("dp", None, None),
        P(),
        P(),
        P(None, "dp"),
        P(None, "dp"),
        P(None, "dp"),
    )
    out_specs = (P("dp", None, None), P(None, "dp"), P(None, "dp"), P(None, "dp"), P())
    return jax.shard_map(
        body, mesh=mesh, in_specs=in_specs, out_specs=out_specs, check_vma=False
    )
```

```python
import functools

import jax
import jax.numpy as jnp
from jax import lax
from jax.experimental import pallas as pl
from jax.experimental.pallas import tpu as pltpu
from jax.sharding import PartitionSpec as P

TILE = 128


filter_rate = 0.3
beta_one = 0.9
beta_two = 0.999
adam_eps = 1e-06
weight_decay = 0.01
learn_rate = 0.01
norm_eps = 1e-06


def take_tiles(source, layer_ids, tile_row, tile_col):

    def single(layer_id, row_tile, col_tile):
        return lax.dynamic_slice(
            source, (layer_id, row_tile * TILE, col_tile * TILE), (1, TILE, TILE)
        )[0]

    return jax.vmap(single)(layer_ids, tile_row, tile_col)


def pack_blocks(grads_dev, memory_dev, layer_ids, tile_row, tile_col):
    grad_tiles = take_tiles(grads_dev, layer_ids, tile_row, tile_col).astype(jnp.float32)
    memory_tiles = take_tiles(memory_dev, layer_ids, tile_row, tile_col).astype(jnp.float32)
    combined = grad_tiles + memory_tiles
    return combined.reshape(combined.shape[0], TILE * TILE)


def selected_mask(layer_ids, block_ids, layers, tile_count):
    columns = layer_ids * (tile_count * tile_count) + block_ids
    all_columns = jnp.arange(layers * tile_count * tile_count, dtype=jnp.int32)
    chosen = jnp.any(columns[:, None] == all_columns[None, :], axis=0)
    return chosen.reshape(layers, tile_count, 1, tile_count, 1)


def filter_memory(grads_dev, memory_dev, chosen):
    layers, model_width, _ = grads_dev.shape
    tile_count = model_width // TILE
    accumulated = grads_dev.astype(jnp.float32) + memory_dev.astype(jnp.float32)
    shaped = accumulated.reshape(layers, tile_count, TILE, tile_count, TILE)
    filtered = jnp.where(chosen, jnp.float32(0.0), shaped).reshape(layers, model_width, model_width)
    mixed = (1.0 - filter_rate) * memory_dev.astype(jnp.float32) + filter_rate * filtered
    return mixed.astype(jnp.bfloat16)


def adam_rows(summed, weights_sel, first_old, second_old):
    first_sel = beta_one * first_old + (1.0 - beta_one) * summed
    second_sel = beta_two * second_old + (1.0 - beta_two) * summed * summed
    update = first_sel / (jnp.sqrt(second_sel) + adam_eps) + weight_decay * weights_sel
    return (first_sel, second_sel, update)


def layer_squares(member, values):
    return jnp.sum(member * jnp.sum(values * values, axis=1)[:, None], axis=0)


def trust_rows(member, weight_total, update_total):
    trust_ratio = jnp.sqrt(weight_total / (update_total + norm_eps))
    return jnp.sum(member * trust_ratio[None, :], axis=1)


def on_device(grads, memory, block_ids, layer_ids, master, first_moment, second_moment):
    layers, model_width, _ = grads.shape
    tile_count = model_width // TILE
    tile_row = block_ids // tile_count
    tile_col = block_ids % tile_count
    columns = layer_ids * (tile_count * tile_count) + block_ids
    member = (layer_ids[:, None] == jnp.arange(layers, dtype=jnp.int32)[None, :]).astype(
        jnp.float32
    )
    weights_sel = jnp.take(master, columns, axis=0)
    first_old = jnp.take(first_moment, columns, axis=0)
    second_old = jnp.take(second_moment, columns, axis=0)
    packed = pack_blocks(grads, memory, layer_ids, tile_row, tile_col)
    summed = lax.psum_scatter(packed, "dp", scatter_dimension=1, tiled=True)
    first_sel, second_sel, update = adam_rows(summed, weights_sel, first_old, second_old)
    weight_total, update_total = lax.psum(
        (layer_squares(member, weights_sel), layer_squares(member, update)), "dp"
    )
    scaled = trust_rows(member, weight_total, update_total)[:, None] * update
    step_blocks = lax.all_gather(scaled.astype(jnp.bfloat16), "dp", axis=1, tiled=True)
    new_memory = filter_memory(
        grads, memory, selected_mask(layer_ids, block_ids, layers, tile_count)
    )
    master_new = master.at[columns].set(weights_sel - learn_rate * scaled)
    first_new = first_moment.at[columns].set(first_sel)
    second_new = second_moment.at[columns].set(second_sel)
    return (new_memory, master_new, first_new, second_new, step_blocks)


def xor_bit(bit, flip):
    return bit if flip == 0 else 1 - bit


def flip_bits(value, flip, size):
    out, weight = 0, 1
    while weight < size:
        bit = lax.rem(lax.div(value, weight), 2)
        out = out + weight * xor_bit(bit, (flip // weight) % 2)
        weight *= 2
    return out


def exchange_kernel(n, layers_hbm, blocks_hbm, grads_hbm, memory_hbm, master_hbm, first_hbm, second_hbm,
                    kept_ref, step_ref, old_ref, rows_ref,
                    layers_smem, blocks_smem, grads_ref, memory_ref, packed, recv1, send2, recv2, send3, recv3,
                    stat_own, stat_in, stat_mid, stat_far, updates, others, state_ref, member_ref, rate_ref,
                    id_sem, load_sem, old_sem, s1, r1, s2, r2, s3, r3, s4, r4, s5, r5, su, ru, sx, rx):
    depth = n // 8
    count = step_ref.shape[0]
    entries = step_ref.shape[1] // n
    pieces = entries // TILE
    lines = pieces * count
    layers, width, _ = grads_ref.shape
    tile_count = width // TILE
    layer_tiles = tile_count * tile_count
    plane_rows = 8 * pieces
    me = lax.axis_index("dp")
    core = lax.rem(me, 2)
    x = lax.rem(lax.div(me, 2), 2)
    y = lax.rem(lax.div(me, 4), 2)
    z = lax.div(me, 8)

    def layer_of(dz):
        return flip_bits(z, dz, depth)

    def plane(dq):
        return xor_bit(y, dq // 2) * 2 + xor_bit(x, dq % 2)

    def device(dz, dq, dc):
        return layer_of(dz) * 8 + plane(dq) * 2 + xor_bit(core, dc)

    def copy(src, dst, send, recv, peer):
        return pltpu.make_async_remote_copy(
            src_ref=src, dst_ref=dst, send_sem=send, recv_sem=recv,
            device_id=(peer,), device_id_type=pl.DeviceIdType.MESH)

    names = [pltpu.make_async_copy(layers_hbm, layers_smem, id_sem.at[0]),
             pltpu.make_async_copy(blocks_hbm, blocks_smem, id_sem.at[1])]
    for name in names:
        name.start()
    loads = []
    parts = load_sem.shape[1]
    step_rows = layers * width // parts
    for i in range(parts):
        layer, rows = i * step_rows // width, pl.ds(i * step_rows % width, step_rows)
        for s, (source, held) in enumerate(((grads_hbm, grads_ref), (memory_hbm, memory_ref))):
            loads.append(pltpu.make_async_copy(source.at[layer, rows], held.at[layer, rows], load_sem.at[s, i]))
            loads[-1].start()

    barrier = pltpu.get_barrier_semaphore()
    peers = [device(0, i // 2, i % 2) for i in range(1, 8)] + [device(dz, 0, 0) for dz in range(1, depth)]
    for peer in peers:
        pl.semaphore_signal(barrier, inc=1, device_id=(peer,), device_id_type=pl.DeviceIdType.MESH)

    for name in names:
        name.wait()
    chosen_layer = [layers_smem[k] for k in range(count)]
    chosen_block = [blocks_smem[k] for k in range(count)]
    columns = [chosen_layer[k] * layer_tiles + chosen_block[k] for k in range(count)]
    shape = (layers * layer_tiles, TILE)
    tile_index = lax.broadcasted_iota(jnp.int32, shape, 0)
    rates = jnp.full(shape, filter_rate, jnp.float32)
    for k in range(count):
        rates = jnp.where(tile_index == columns[k], jnp.float32(0.0), rates)
    rate_ref[...] = rates
    order_index = lax.rem(lax.broadcasted_iota(jnp.int32, (lines, TILE), 0), count)
    line_layer = jnp.zeros((lines, TILE), jnp.int32)
    for k in range(count):
        line_layer = jnp.where(order_index == k, chosen_layer[k], line_layer)
    for l in range(layers):
        member_ref[l] = jnp.where(line_layer == l, jnp.float32(1.0), jnp.float32(0.0))
    stat_own[...] = jnp.zeros_like(stat_own)

    def filter_slabs(start, stop):
        @pl.loop(start, stop)
        def _(i):
            layer = lax.div(i, tile_count)
            rows = pl.ds(pl.multiple_of(lax.rem(i, tile_count) * TILE, TILE), TILE)
            for t in range(tile_count):
                lanes = slice(t * TILE, (t + 1) * TILE)
                rate = rate_ref[pl.ds(i * tile_count + t, 1), :]
                mixed = (rate + (1.0 - filter_rate)) * memory_ref[layer, rows, lanes].astype(jnp.float32)
                mixed = mixed + rate * grads_ref[layer, rows, lanes].astype(jnp.float32)
                kept_ref[layer, rows, lanes] = mixed.astype(kept_ref.dtype)

    slabs = layers * tile_count

    for load in loads:
        load.wait()
    pl.semaphore_wait(barrier, len(peers))

    far = list(range(depth - 1, -1, -1))
    order = (3, 1, 2, 0)
    first_hop, second_hop, third_hop = {}, {}, {}
    for dz in far:
        at = layer_of(dz)
        for k in range(count):
            rows = pl.ds((lax.div(chosen_block[k], tile_count) * depth + at) * plane_rows, plane_rows)
            lanes = pl.ds(lax.rem(chosen_block[k], tile_count) * TILE, TILE)
            packed[dz, pl.ds(k, plane_rows, stride=count), :] = (
                grads_ref[chosen_layer[k], rows, lanes].astype(jnp.float32)
                + memory_ref[chosen_layer[k], rows, lanes].astype(jnp.float32))
        for dq in order:
            slot = dz * 4 + dq
            first_hop[slot] = copy(packed.at[dz, chunk_lines(plane(dq), 1 - core, lines)], recv1.at[slot],
                                   s1.at[slot], r1.at[slot], device(0, 0, 1))
            first_hop[slot].start()
    olds = []
    for s, source in enumerate((master_hbm, first_hbm, second_hbm)):
        olds.append(pltpu.make_async_copy(source, old_ref.at[s], old_sem.at[s]))
        olds[-1].start()
    def own(dz, dq):
        return packed[dz, chunk_lines(plane(dq), core, lines), :]

    for dz in far:
        for dq in order[:3]:
            slot, place = dz * 4 + dq, dz * 3 + dq - 1
            first_hop[slot].wait_recv()
            send2[place] = own(dz, dq) + recv1[slot]
            second_hop[place] = copy(send2.at[place], recv2.at[place], s2.at[place], r2.at[place], device(0, dq, 0))
            second_hop[place].start()

    for old in olds:
        old.wait()
    for s in range(3):
        for k in range(count):
            line = old_ref[s, pl.ds(columns[k], 1), :]
            for j in range(pieces):
                state_ref[s, j * count + k:j * count + k + 1, :] = line[:, j * TILE:(j + 1) * TILE]
    weights = state_ref[0]
    for l in range(layers):
        stat_own[l:l + 1, :] = jnp.sum(member_ref[l] * (weights * weights), axis=0, keepdims=True)
    filter_slabs(0, slabs // 2)

    summed = None
    for dz in far:
        first_hop[dz * 4].wait_recv()
        for dq in range(3):
            second_hop[dz * 3 + dq].wait_recv()
        part = (own(dz, 0) + recv1[dz * 4]) + ((recv2[dz * 3] + recv2[dz * 3 + 1]) + recv2[dz * 3 + 2])
        if dz == 0:
            summed = part
        else:
            send3[dz - 1] = part
            third_hop[dz] = copy(send3.at[dz - 1], recv3.at[dz - 1], s3.at[dz - 1], r3.at[dz - 1], device(dz, 0, 0))
            third_hop[dz].start()
    for dz in range(1, depth):
        third_hop[dz].wait_recv()
        summed = summed + recv3[dz - 1]

    first_sel = beta_one * state_ref[1] + (1.0 - beta_one) * summed
    second_sel = beta_two * state_ref[2] + (1.0 - beta_two) * summed * summed
    update = first_sel / (jnp.sqrt(second_sel) + adam_eps) + weight_decay * weights
    updates[0] = update
    ahead, across, near, away = {}, {}, [], []

    def lift(dz, dq, to_z, to_q, send, at):
        ahead[dz * 4 + dq] = copy(updates.at[at], updates.at[dz * 4 + dq], send, ru.at[dz * 4 + dq], device(to_z, to_q, 0))
        ahead[dz * 4 + dq].start()

    def cross(slot):
        across[slot] = copy(updates.at[slot], others.at[slot], sx.at[slot], rx.at[slot], device(0, 0, 1))
        across[slot].start()

    for dz in far[:-1]:
        lift(dz, 0, dz, 0, su.at[dz * 4], 0)
    for dq in order[:3]:
        lift(0, dq, 0, dq, su.at[dq], 0)
    for l in range(layers):
        stat_own[layers + l:layers + l + 1, :] = jnp.sum(member_ref[l] * (update * update), axis=0, keepdims=True)

    def spot(i):
        return plane(i // 2) * 2 + xor_bit(core, i % 2)

    for i in range(1, 8):
        near.append(copy(stat_own, stat_in.at[spot(0)], s4.at[i - 1], r4.at[i - 1], device(0, i // 2, i % 2)))
        near[-1].start()
    cross(0)
    rows_ref[1] = first_sel
    rows_ref[2] = second_sel
    stat_in[spot(0)] = stat_own[...]
    filter_slabs(slabs // 2, slabs)
    for hops in (first_hop, second_hop, third_hop):
        for hop in hops.values():
            hop.wait_send()
    ahead[4].wait_recv()
    for dq in order[:3]:
        lift(1, dq, 0, dq, su.at[4 + dq], 4)
    cross(4)
    for i in range(1, 8):
        copy(stat_own, stat_in.at[spot(i)], s4.at[i - 1], r4.at[i - 1], device(0, i // 2, i % 2)).wait_recv()
    total = stat_in[0]
    for i in range(1, 8):
        total = total + stat_in[i]
    stat_mid[...] = total
    for dz in range(1, depth):
        away.append(copy(stat_mid, stat_far.at[z], s5.at[dz - 1], r5.at[dz - 1], device(dz, 0, 0)))
        away[-1].start()
    stat_far[z] = total
    for dz in range(2, depth):
        ahead[dz * 4].wait_recv()
        for dq in order[:3]:
            lift(dz, dq, 0, dq, su.at[dz * 4 + dq], dz * 4)
        cross(dz * 4)
    for dq in order[:3]:
        ahead[dq].wait_recv()
        cross(dq)
    for dz in range(1, depth):
        copy(stat_mid, stat_far.at[layer_of(dz)], s5.at[dz - 1], r5.at[dz - 1], device(dz, 0, 0)).wait_recv()
    total = stat_far[0]
    for at in range(1, depth):
        total = total + stat_far[at]
    sums = jnp.sum(total, axis=1, keepdims=True)
    factor = jnp.zeros_like(update)
    for l in range(layers):
        ratio = jnp.sqrt(sums[l:l + 1] / (sums[layers + l:layers + l + 1] + norm_eps))
        factor = factor + member_ref[l] * ratio
    rows_ref[0] = weights - learn_rate * (factor * update)

    def place(source, dz, dq, part):
        scaled = factor * source[dz * 4 + dq]
        owner = layer_of(dz) * 8 + plane(dq) * 2 + part
        for j in range(pieces):
            lanes = pl.ds(pl.multiple_of(owner * entries + j * TILE, TILE), TILE)
            step_ref[:, lanes] = scaled[j * count:(j + 1) * count].astype(step_ref.dtype)

    def mine(dz, dq):
        place(updates, dz, dq, core)

    def theirs(dz, dq):
        across[dz * 4 + dq].wait_recv()
        place(others, dz, dq, 1 - core)

    for dz in range(depth):
        mine(dz, 0)
    for dq in order[:3]:
        mine(0, dq)
    for dq in (0,) + order[:3]:
        theirs(0, dq)
    for hop in near + away:
        hop.wait_send()
    for dz in range(1, depth):
        theirs(dz, 0)
    for dz in range(1, depth):
        for dq in order[:3]:
            ahead[dz * 4 + dq].wait_recv()
            cross(dz * 4 + dq)
            mine(dz, dq)
        if dz > 1:
            for dq in order[:3]:
                theirs(dz - 1, dq)
    last = [(depth - 1) * 4 + dq for dq in order[:3]]
    for hop in ahead.values():
        hop.wait_send()
    for slot, hop in across.items():
        if slot not in last:
            hop.wait_send()
    for dq in order[:3]:
        theirs(depth - 1, dq)
    for slot in last:
        across[slot].wait_send()


def chunk_lines(plane_at, part, lines):
    return pl.ds(pl.multiple_of((plane_at * 2 + part) * lines, lines), lines)


def state_kernel(layers_hbm, blocks_hbm, kept_ref, step_ref, old_ref, rows_ref,
                 kept_out, master_out, first_out, second_out, step_out,
                 layers_smem, blocks_smem, new_ref, sem):
    count = layers_smem.shape[0]
    names = [pltpu.make_async_copy(layers_hbm, layers_smem, sem.at[0]),
             pltpu.make_async_copy(blocks_hbm, blocks_smem, sem.at[1])]
    for name in names:
        name.start()
    pieces = rows_ref.shape[1] // count
    layers, width, _ = kept_ref.shape
    layer_rows = (width // TILE) * (width // TILE)
    outs = [pltpu.make_async_copy(kept_ref.at[l], kept_out.at[l], sem.at[6 + l]) for l in range(layers)]
    outs.append(pltpu.make_async_copy(step_ref, step_out, sem.at[5]))
    for out in outs:
        out.start()
    for name in names:
        name.wait()
    for s, target in enumerate((master_out, first_out, second_out)):
        new_ref[s] = old_ref[s]
        for k in range(count):
            column = layers_smem[k] * layer_rows + blocks_smem[k]
            base = pl.ds(pl.multiple_of(lax.div(column, 8) * 8, 8), 8)
            hit = lax.broadcasted_iota(jnp.int32, (8, TILE), 0) == lax.rem(column, 8)
            for j in range(pieces):
                lanes = slice(j * TILE, (j + 1) * TILE)
                line = rows_ref[s, j * count + k:j * count + k + 1, :]
                new_ref[s, base, lanes] = jnp.where(hit, line, new_ref[s, base, lanes])
        outs.append(pltpu.make_async_copy(new_ref.at[s], target, sem.at[2 + s]))
        outs[-1].start()
    for out in outs:
        out.wait()


def on_device_kernels(n, grads, memory, block_ids, layer_ids, master, first_moment, second_moment):
    layers, width, _ = grads.shape
    tile_count = width // TILE
    count = block_ids.shape[0]
    entries = master.shape[1]
    lines = entries // TILE * count
    depth = n // 8
    f32 = jnp.float32
    vmem, hbm = (pl.BlockSpec(memory_space=m) for m in (pltpu.VMEM, pltpu.HBM))
    dma = pltpu.SemaphoreType.DMA
    stat_rows = -(-2 * layers // 8) * 8

    def chunks(*lead):
        return pltpu.VMEM(lead + (lines, TILE), f32)

    grads, memory, block_ids, layer_ids, master, first_moment, second_moment = (
        pltpu.with_memory_space_constraint(v, pltpu.HBM)
        for v in (grads, memory, block_ids, layer_ids, master, first_moment, second_moment))
    kept, step, old, rows = pl.pallas_call(
        functools.partial(exchange_kernel, n),
        out_shape=[pltpu.VMEM(memory.shape, jnp.bfloat16),
                   pltpu.VMEM((count, n * entries), jnp.bfloat16),
                   pltpu.VMEM((3,) + master.shape, f32),
                   chunks(3)],
        in_specs=[hbm] * 7,
        out_specs=[vmem] * 4,
        scratch_shapes=[
            pltpu.SMEM((count,), jnp.int32), pltpu.SMEM((count,), jnp.int32),
            pltpu.VMEM(grads.shape, jnp.bfloat16), pltpu.VMEM(memory.shape, jnp.bfloat16),
            pltpu.VMEM((depth, 8 * lines, TILE), f32),
            chunks(depth * 4), chunks(depth * 3), chunks(depth * 3), chunks(depth - 1), chunks(depth - 1),
            pltpu.VMEM((stat_rows, TILE), f32),
            pltpu.VMEM((8, stat_rows, TILE), f32),
            pltpu.VMEM((stat_rows, TILE), f32),
            pltpu.VMEM((depth, stat_rows, TILE), f32),
            chunks(depth * 4), chunks(depth * 4), chunks(3), chunks(layers),
            pltpu.VMEM((layers * tile_count * tile_count, TILE), f32),
            dma((2,)), dma((2, 4 * layers)), dma((3,)),
            dma((depth * 4,)), dma((depth * 4,)), dma((depth * 3,)), dma((depth * 3,)), dma((depth - 1,)), dma((depth - 1,)),
            dma((7,)), dma((7,)), dma((depth - 1,)), dma((depth - 1,)),
            dma((depth * 4,)), dma((depth * 4,)), dma((depth * 4,)), dma((depth * 4,))],
        compiler_params=pltpu.CompilerParams(collective_id=0, has_side_effects=True, vmem_limit_bytes=40 * 2 ** 20),
        name="exchange",
    )(layer_ids, block_ids, grads, memory, master, first_moment, second_moment)
    like = jax.ShapeDtypeStruct(master.shape, f32)
    new_memory, master_new, first_new, second_new, step_blocks = pl.pallas_call(
        state_kernel,
        out_shape=[jax.ShapeDtypeStruct(memory.shape, jnp.bfloat16)] + [like] * 3
        + [jax.ShapeDtypeStruct(step.shape, jnp.bfloat16)],
        in_specs=[hbm, hbm] + [vmem] * 4,
        out_specs=[hbm] * 5,
        scratch_shapes=[pltpu.SMEM((count,), jnp.int32), pltpu.SMEM((count,), jnp.int32),
                        pltpu.VMEM((3,) + master.shape, f32), dma((6 + layers,))],
        compiler_params=pltpu.CompilerParams(vmem_limit_bytes=16 * 2 ** 20),
        name="state",
    )(layer_ids, block_ids, kept, step, old, rows)
    return (new_memory, master_new, first_new, second_new, step_blocks)


def solution(mesh):
    n = mesh.shape["dp"]
    depth = n // 8

    def body(*args):
        entries, count = args[4].shape[1], args[2].shape[0]
        if n % 8 == 0 and depth > 1 and depth & (depth - 1) == 0 and entries % TILE == 0 and count % 16 == 0:
            return on_device_kernels(n, *args)
        return on_device(*args)

    in_specs = (
        P("dp", None, None),
        P("dp", None, None),
        P(),
        P(),
        P(None, "dp"),
        P(None, "dp"),
        P(None, "dp"),
    )
    out_specs = (P("dp", None, None), P(None, "dp"), P(None, "dp"), P(None, "dp"), P())
    return jax.shard_map(
        body, mesh=mesh, in_specs=in_specs, out_specs=out_specs, check_vma=False
    )
```

```python
import functools

import jax
import jax.numpy as jnp
from jax import lax
from jax.experimental import pallas as pl
from jax.experimental.pallas import tpu as pltpu
from jax.sharding import PartitionSpec as P

TILE = 128


filter_rate = 0.3
beta_one = 0.9
beta_two = 0.999
adam_eps = 1e-06
weight_decay = 0.01
learn_rate = 0.01
norm_eps = 1e-06


def take_tiles(source, layer_ids, tile_row, tile_col):

    def single(layer_id, row_tile, col_tile):
        return lax.dynamic_slice(
            source, (layer_id, row_tile * TILE, col_tile * TILE), (1, TILE, TILE)
        )[0]

    return jax.vmap(single)(layer_ids, tile_row, tile_col)


def pack_blocks(grads_dev, memory_dev, layer_ids, tile_row, tile_col):
    grad_tiles = take_tiles(grads_dev, layer_ids, tile_row, tile_col).astype(jnp.float32)
    memory_tiles = take_tiles(memory_dev, layer_ids, tile_row, tile_col).astype(jnp.float32)
    combined = grad_tiles + memory_tiles
    return combined.reshape(combined.shape[0], TILE * TILE)


def selected_mask(layer_ids, block_ids, layers, tile_count):
    columns = layer_ids * (tile_count * tile_count) + block_ids
    all_columns = jnp.arange(layers * tile_count * tile_count, dtype=jnp.int32)
    chosen = jnp.any(columns[:, None] == all_columns[None, :], axis=0)
    return chosen.reshape(layers, tile_count, 1, tile_count, 1)


def filter_memory(grads_dev, memory_dev, chosen):
    layers, model_width, _ = grads_dev.shape
    tile_count = model_width // TILE
    accumulated = grads_dev.astype(jnp.float32) + memory_dev.astype(jnp.float32)
    shaped = accumulated.reshape(layers, tile_count, TILE, tile_count, TILE)
    filtered = jnp.where(chosen, jnp.float32(0.0), shaped).reshape(layers, model_width, model_width)
    mixed = (1.0 - filter_rate) * memory_dev.astype(jnp.float32) + filter_rate * filtered
    return mixed.astype(jnp.bfloat16)


def adam_rows(summed, weights_sel, first_old, second_old):
    first_sel = beta_one * first_old + (1.0 - beta_one) * summed
    second_sel = beta_two * second_old + (1.0 - beta_two) * summed * summed
    update = first_sel / (jnp.sqrt(second_sel) + adam_eps) + weight_decay * weights_sel
    return (first_sel, second_sel, update)


def layer_squares(member, values):
    return jnp.sum(member * jnp.sum(values * values, axis=1)[:, None], axis=0)


def trust_rows(member, weight_total, update_total):
    trust_ratio = jnp.sqrt(weight_total / (update_total + norm_eps))
    return jnp.sum(member * trust_ratio[None, :], axis=1)


def on_device(grads, memory, block_ids, layer_ids, master, first_moment, second_moment):
    layers, model_width, _ = grads.shape
    tile_count = model_width // TILE
    tile_row = block_ids // tile_count
    tile_col = block_ids % tile_count
    columns = layer_ids * (tile_count * tile_count) + block_ids
    member = (layer_ids[:, None] == jnp.arange(layers, dtype=jnp.int32)[None, :]).astype(
        jnp.float32
    )
    weights_sel = jnp.take(master, columns, axis=0)
    first_old = jnp.take(first_moment, columns, axis=0)
    second_old = jnp.take(second_moment, columns, axis=0)
    packed = pack_blocks(grads, memory, layer_ids, tile_row, tile_col)
    summed = lax.psum_scatter(packed, "dp", scatter_dimension=1, tiled=True)
    first_sel, second_sel, update = adam_rows(summed, weights_sel, first_old, second_old)
    weight_total, update_total = lax.psum(
        (layer_squares(member, weights_sel), layer_squares(member, update)), "dp"
    )
    scaled = trust_rows(member, weight_total, update_total)[:, None] * update
    step_blocks = lax.all_gather(scaled.astype(jnp.bfloat16), "dp", axis=1, tiled=True)
    new_memory = filter_memory(
        grads, memory, selected_mask(layer_ids, block_ids, layers, tile_count)
    )
    master_new = master.at[columns].set(weights_sel - learn_rate * scaled)
    first_new = first_moment.at[columns].set(first_sel)
    second_new = second_moment.at[columns].set(second_sel)
    return (new_memory, master_new, first_new, second_new, step_blocks)


def xor_bit(bit, flip):
    return bit if flip == 0 else 1 - bit


def flip_bits(value, flip, size):
    out, weight = 0, 1
    while weight < size:
        bit = lax.rem(lax.div(value, weight), 2)
        out = out + weight * xor_bit(bit, (flip // weight) % 2)
        weight *= 2
    return out


def exchange_kernel(n, layers_hbm, blocks_hbm, grads_hbm, memory_hbm, master_hbm, first_hbm, second_hbm,
                    kept_ref, step_ref, old_ref, rows_ref,
                    layers_smem, blocks_smem, grads_ref, memory_ref, packed, recv1, send2, recv2, send3, recv3,
                    stat_own, stat_in, stat_mid, stat_far, updates, others, state_ref, member_ref, rate_ref,
                    id_sem, load_sem, old_sem, s1, r1, s2, r2, s3, r3, s4, r4, s5, r5, su, ru, sx, rx):
    depth = n // 8
    count = step_ref.shape[0]
    entries = step_ref.shape[1] // n
    pieces = entries // TILE
    lines = pieces * count
    layers, width, _ = grads_ref.shape
    tile_count = width // TILE
    layer_tiles = tile_count * tile_count
    plane_rows = 8 * pieces
    me = lax.axis_index("dp")
    core = lax.rem(me, 2)
    x = lax.rem(lax.div(me, 2), 2)
    y = lax.rem(lax.div(me, 4), 2)
    z = lax.div(me, 8)

    def layer_of(dz):
        return flip_bits(z, dz, depth)

    def plane(dq):
        return xor_bit(y, dq // 2) * 2 + xor_bit(x, dq % 2)

    def device(dz, dq, dc):
        return layer_of(dz) * 8 + plane(dq) * 2 + xor_bit(core, dc)

    def copy(src, dst, send, recv, peer):
        return pltpu.make_async_remote_copy(
            src_ref=src, dst_ref=dst, send_sem=send, recv_sem=recv,
            device_id=(peer,), device_id_type=pl.DeviceIdType.MESH)

    names = [pltpu.make_async_copy(layers_hbm, layers_smem, id_sem.at[0]),
             pltpu.make_async_copy(blocks_hbm, blocks_smem, id_sem.at[1])]
    for name in names:
        name.start()
    loads = []
    parts = load_sem.shape[1]
    step_rows = layers * width // parts
    for i in range(parts):
        layer, rows = i * step_rows // width, pl.ds(i * step_rows % width, step_rows)
        for s, (source, held) in enumerate(((grads_hbm, grads_ref), (memory_hbm, memory_ref))):
            loads.append(pltpu.make_async_copy(source.at[layer, rows], held.at[layer, rows], load_sem.at[s, i]))
            loads[-1].start()

    barrier = pltpu.get_barrier_semaphore()
    peers = [device(0, i // 2, i % 2) for i in range(1, 8)] + [device(dz, 0, 0) for dz in range(1, depth)]
    for peer in peers:
        pl.semaphore_signal(barrier, inc=1, device_id=(peer,), device_id_type=pl.DeviceIdType.MESH)

    for name in names:
        name.wait()
    chosen_layer = [layers_smem[k] for k in range(count)]
    chosen_block = [blocks_smem[k] for k in range(count)]
    columns = [chosen_layer[k] * layer_tiles + chosen_block[k] for k in range(count)]
    shape = (layers * layer_tiles, TILE)
    tile_index = lax.broadcasted_iota(jnp.int32, shape, 0)
    rates = jnp.full(shape, filter_rate, jnp.float32)
    for k in range(count):
        rates = jnp.where(tile_index == columns[k], jnp.float32(0.0), rates)
    rate_ref[...] = rates
    order_index = lax.rem(lax.broadcasted_iota(jnp.int32, (lines, TILE), 0), count)
    line_layer = jnp.zeros((lines, TILE), jnp.int32)
    for k in range(count):
        line_layer = jnp.where(order_index == k, chosen_layer[k], line_layer)
    for l in range(layers):
        member_ref[l] = jnp.where(line_layer == l, jnp.float32(1.0), jnp.float32(0.0))
    stat_own[...] = jnp.zeros_like(stat_own)

    def filter_slabs(start, stop):
        @pl.loop(start, stop)
        def _(i):
            layer = lax.div(i, tile_count)
            rows = pl.ds(pl.multiple_of(lax.rem(i, tile_count) * TILE, TILE), TILE)
            for t in range(tile_count):
                lanes = slice(t * TILE, (t + 1) * TILE)
                rate = rate_ref[pl.ds(i * tile_count + t, 1), :]
                mixed = (rate + (1.0 - filter_rate)) * memory_ref[layer, rows, lanes].astype(jnp.float32)
                mixed = mixed + rate * grads_ref[layer, rows, lanes].astype(jnp.float32)
                kept_ref[layer, rows, lanes] = mixed.astype(kept_ref.dtype)

    slabs = layers * tile_count

    for load in loads:
        load.wait()
    pl.semaphore_wait(barrier, len(peers))

    far = list(range(depth - 1, -1, -1))
    order = (3, 1, 2, 0)
    first_hop, second_hop, third_hop = {}, {}, {}
    def pack(dz):
        at = layer_of(dz)
        for k in range(count):
            rows = pl.ds((lax.div(chosen_block[k], tile_count) * depth + at) * plane_rows, plane_rows)
            lanes = pl.ds(lax.rem(chosen_block[k], tile_count) * TILE, TILE)
            packed[dz, pl.ds(k, plane_rows, stride=count), :] = (
                grads_ref[chosen_layer[k], rows, lanes].astype(jnp.float32)
                + memory_ref[chosen_layer[k], rows, lanes].astype(jnp.float32))
        for dq in order:
            slot = dz * 4 + dq
            first_hop[slot] = copy(packed.at[dz, chunk_lines(plane(dq), 1 - core, lines)], recv1.at[slot],
                                   s1.at[slot], r1.at[slot], device(0, 0, 1))
            first_hop[slot].start()

    def own(dz, dq):
        return packed[dz, chunk_lines(plane(dq), core, lines), :]

    def spread(dz):
        for dq in order[:3]:
            slot, place = dz * 4 + dq, dz * 3 + dq - 1
            first_hop[slot].wait_recv()
            send2[place] = own(dz, dq) + recv1[slot]
            second_hop[place] = copy(send2.at[place], recv2.at[place], s2.at[place], r2.at[place], device(0, dq, 0))
            second_hop[place].start()

    for i, dz in enumerate(far):
        pack(dz)
        if i >= 2:
            spread(far[i - 2])
    olds = []
    for s, source in enumerate((master_hbm, first_hbm, second_hbm)):
        olds.append(pltpu.make_async_copy(source, old_ref.at[s], old_sem.at[s]))
        olds[-1].start()
    for dz in far[-2:]:
        spread(dz)

    for old in olds:
        old.wait()
    for s in range(3):
        for k in range(count):
            line = old_ref[s, pl.ds(columns[k], 1), :]
            for j in range(pieces):
                state_ref[s, j * count + k:j * count + k + 1, :] = line[:, j * TILE:(j + 1) * TILE]
    weights = state_ref[0]
    for l in range(layers):
        stat_own[l:l + 1, :] = jnp.sum(member_ref[l] * (weights * weights), axis=0, keepdims=True)
    filter_slabs(0, slabs // 2)

    summed = None
    for dz in far:
        first_hop[dz * 4].wait_recv()
        for dq in range(3):
            second_hop[dz * 3 + dq].wait_recv()
        part = (own(dz, 0) + recv1[dz * 4]) + ((recv2[dz * 3] + recv2[dz * 3 + 1]) + recv2[dz * 3 + 2])
        if dz == 0:
            summed = part
        else:
            send3[dz - 1] = part
            third_hop[dz] = copy(send3.at[dz - 1], recv3.at[dz - 1], s3.at[dz - 1], r3.at[dz - 1], device(dz, 0, 0))
            third_hop[dz].start()
    for dz in range(1, depth):
        third_hop[dz].wait_recv()
        summed = summed + recv3[dz - 1]

    first_sel = beta_one * state_ref[1] + (1.0 - beta_one) * summed
    second_sel = beta_two * state_ref[2] + (1.0 - beta_two) * summed * summed
    update = first_sel / (jnp.sqrt(second_sel) + adam_eps) + weight_decay * weights
    updates[0] = update
    ahead, across, near, away = {}, {}, [], []

    def lift(dz, dq, to_z, to_q, send, at):
        ahead[dz * 4 + dq] = copy(updates.at[at], updates.at[dz * 4 + dq], send, ru.at[dz * 4 + dq], device(to_z, to_q, 0))
        ahead[dz * 4 + dq].start()

    def cross(slot):
        across[slot] = copy(updates.at[slot], others.at[slot], sx.at[slot], rx.at[slot], device(0, 0, 1))
        across[slot].start()

    for dz in far[:-1]:
        lift(dz, 0, dz, 0, su.at[dz * 4], 0)
    for dq in order[:3]:
        lift(0, dq, 0, dq, su.at[dq], 0)
    for l in range(layers):
        stat_own[layers + l:layers + l + 1, :] = jnp.sum(member_ref[l] * (update * update), axis=0, keepdims=True)

    def spot(i):
        return plane(i // 2) * 2 + xor_bit(core, i % 2)

    for i in range(1, 8):
        near.append(copy(stat_own, stat_in.at[spot(0)], s4.at[i - 1], r4.at[i - 1], device(0, i // 2, i % 2)))
        near[-1].start()
    cross(0)
    rows_ref[1] = first_sel
    rows_ref[2] = second_sel
    stat_in[spot(0)] = stat_own[...]
    filter_slabs(slabs // 2, slabs)
    for hops in (first_hop, second_hop, third_hop):
        for hop in hops.values():
            hop.wait_send()
    ahead[4].wait_recv()
    for dq in order[:3]:
        lift(1, dq, 0, dq, su.at[4 + dq], 4)
    cross(4)
    for i in range(1, 8):
        copy(stat_own, stat_in.at[spot(i)], s4.at[i - 1], r4.at[i - 1], device(0, i // 2, i % 2)).wait_recv()
    total = stat_in[0]
    for i in range(1, 8):
        total = total + stat_in[i]
    stat_mid[...] = total
    for dz in range(1, depth):
        away.append(copy(stat_mid, stat_far.at[z], s5.at[dz - 1], r5.at[dz - 1], device(dz, 0, 0)))
        away[-1].start()
    stat_far[z] = total
    for dz in range(2, depth):
        ahead[dz * 4].wait_recv()
        for dq in order[:3]:
            lift(dz, dq, 0, dq, su.at[dz * 4 + dq], dz * 4)
        cross(dz * 4)
    for dq in order[:3]:
        ahead[dq].wait_recv()
        cross(dq)
    for dz in range(1, depth):
        copy(stat_mid, stat_far.at[layer_of(dz)], s5.at[dz - 1], r5.at[dz - 1], device(dz, 0, 0)).wait_recv()
    total = stat_far[0]
    for at in range(1, depth):
        total = total + stat_far[at]
    sums = jnp.sum(total, axis=1, keepdims=True)
    factor = jnp.zeros_like(update)
    for l in range(layers):
        ratio = jnp.sqrt(sums[l:l + 1] / (sums[layers + l:layers + l + 1] + norm_eps))
        factor = factor + member_ref[l] * ratio
    rows_ref[0] = weights - learn_rate * (factor * update)

    def place(source, dz, dq, part):
        scaled = factor * source[dz * 4 + dq]
        owner = layer_of(dz) * 8 + plane(dq) * 2 + part
        for j in range(pieces):
            lanes = pl.ds(pl.multiple_of(owner * entries + j * TILE, TILE), TILE)
            step_ref[:, lanes] = scaled[j * count:(j + 1) * count].astype(step_ref.dtype)

    def mine(dz, dq):
        place(updates, dz, dq, core)

    def theirs(dz, dq):
        across[dz * 4 + dq].wait_recv()
        place(others, dz, dq, 1 - core)

    for dz in range(depth):
        mine(dz, 0)
    for dq in order[:3]:
        mine(0, dq)
    for dq in (0,) + order[:3]:
        theirs(0, dq)
    for hop in near + away:
        hop.wait_send()
    for dz in range(1, depth):
        for dq in order[:3]:
            ahead[dz * 4 + dq].wait_recv()
            cross(dz * 4 + dq)
            mine(dz, dq)
        theirs(dz, 0)
        if dz > 1:
            for dq in order[:3]:
                theirs(dz - 1, dq)
    for hop in ahead.values():
        hop.wait_send()
    for dq in order[:3]:
        theirs(depth - 1, dq)
    for hop in across.values():
        hop.wait_send()


def chunk_lines(plane_at, part, lines):
    return pl.ds(pl.multiple_of((plane_at * 2 + part) * lines, lines), lines)


def state_kernel(layers_hbm, blocks_hbm, kept_ref, step_ref, old_ref, rows_ref,
                 kept_out, master_out, first_out, second_out, step_out,
                 layers_smem, blocks_smem, new_ref, sem):
    count = layers_smem.shape[0]
    names = [pltpu.make_async_copy(layers_hbm, layers_smem, sem.at[0]),
             pltpu.make_async_copy(blocks_hbm, blocks_smem, sem.at[1])]
    for name in names:
        name.start()
    pieces = rows_ref.shape[1] // count
    layers, width, _ = kept_ref.shape
    layer_rows = (width // TILE) * (width // TILE)
    outs = [pltpu.make_async_copy(kept_ref.at[l], kept_out.at[l], sem.at[6 + l]) for l in range(layers)]
    outs.append(pltpu.make_async_copy(step_ref, step_out, sem.at[5]))
    for out in outs:
        out.start()
    for name in names:
        name.wait()
    for s, target in enumerate((master_out, first_out, second_out)):
        new_ref[s] = old_ref[s]
        for k in range(count):
            column = layers_smem[k] * layer_rows + blocks_smem[k]
            base = pl.ds(pl.multiple_of(lax.div(column, 8) * 8, 8), 8)
            hit = lax.broadcasted_iota(jnp.int32, (8, TILE), 0) == lax.rem(column, 8)
            for j in range(pieces):
                lanes = slice(j * TILE, (j + 1) * TILE)
                line = rows_ref[s, j * count + k:j * count + k + 1, :]
                new_ref[s, base, lanes] = jnp.where(hit, line, new_ref[s, base, lanes])
        outs.append(pltpu.make_async_copy(new_ref.at[s], target, sem.at[2 + s]))
        outs[-1].start()
    for out in outs:
        out.wait()


def on_device_kernels(n, grads, memory, block_ids, layer_ids, master, first_moment, second_moment):
    layers, width, _ = grads.shape
    tile_count = width // TILE
    count = block_ids.shape[0]
    entries = master.shape[1]
    lines = entries // TILE * count
    depth = n // 8
    f32 = jnp.float32
    vmem, hbm = (pl.BlockSpec(memory_space=m) for m in (pltpu.VMEM, pltpu.HBM))
    dma = pltpu.SemaphoreType.DMA
    stat_rows = -(-2 * layers // 8) * 8

    def chunks(*lead):
        return pltpu.VMEM(lead + (lines, TILE), f32)

    grads, memory, block_ids, layer_ids, master, first_moment, second_moment = (
        pltpu.with_memory_space_constraint(v, pltpu.HBM)
        for v in (grads, memory, block_ids, layer_ids, master, first_moment, second_moment))
    kept, step, old, rows = pl.pallas_call(
        functools.partial(exchange_kernel, n),
        out_shape=[pltpu.VMEM(memory.shape, jnp.bfloat16),
                   pltpu.VMEM((count, n * entries), jnp.bfloat16),
                   pltpu.VMEM((3,) + master.shape, f32),
                   chunks(3)],
        in_specs=[hbm] * 7,
        out_specs=[vmem] * 4,
        scratch_shapes=[
            pltpu.SMEM((count,), jnp.int32), pltpu.SMEM((count,), jnp.int32),
            pltpu.VMEM(grads.shape, jnp.bfloat16), pltpu.VMEM(memory.shape, jnp.bfloat16),
            pltpu.VMEM((depth, 8 * lines, TILE), f32),
            chunks(depth * 4), chunks(depth * 3), chunks(depth * 3), chunks(depth - 1), chunks(depth - 1),
            pltpu.VMEM((stat_rows, TILE), f32),
            pltpu.VMEM((8, stat_rows, TILE), f32),
            pltpu.VMEM((stat_rows, TILE), f32),
            pltpu.VMEM((depth, stat_rows, TILE), f32),
            chunks(depth * 4), chunks(depth * 4), chunks(3), chunks(layers),
            pltpu.VMEM((layers * tile_count * tile_count, TILE), f32),
            dma((2,)), dma((2, 4 * layers)), dma((3,)),
            dma((depth * 4,)), dma((depth * 4,)), dma((depth * 3,)), dma((depth * 3,)), dma((depth - 1,)), dma((depth - 1,)),
            dma((7,)), dma((7,)), dma((depth - 1,)), dma((depth - 1,)),
            dma((depth * 4,)), dma((depth * 4,)), dma((depth * 4,)), dma((depth * 4,))],
        compiler_params=pltpu.CompilerParams(collective_id=0, has_side_effects=True, vmem_limit_bytes=40 * 2 ** 20),
        name="exchange",
    )(layer_ids, block_ids, grads, memory, master, first_moment, second_moment)
    like = jax.ShapeDtypeStruct(master.shape, f32)
    new_memory, master_new, first_new, second_new, step_blocks = pl.pallas_call(
        state_kernel,
        out_shape=[jax.ShapeDtypeStruct(memory.shape, jnp.bfloat16)] + [like] * 3
        + [jax.ShapeDtypeStruct(step.shape, jnp.bfloat16)],
        in_specs=[hbm, hbm] + [vmem] * 4,
        out_specs=[hbm] * 5,
        scratch_shapes=[pltpu.SMEM((count,), jnp.int32), pltpu.SMEM((count,), jnp.int32),
                        pltpu.VMEM((3,) + master.shape, f32), dma((6 + layers,))],
        compiler_params=pltpu.CompilerParams(vmem_limit_bytes=16 * 2 ** 20),
        name="state",
    )(layer_ids, block_ids, kept, step, old, rows)
    return (new_memory, master_new, first_new, second_new, step_blocks)


def solution(mesh):
    n = mesh.shape["dp"]
    depth = n // 8

    def body(*args):
        entries, count = args[4].shape[1], args[2].shape[0]
        if n % 8 == 0 and depth > 1 and depth & (depth - 1) == 0 and entries % TILE == 0 and count % 16 == 0:
            return on_device_kernels(n, *args)
        return on_device(*args)

    in_specs = (
        P("dp", None, None),
        P("dp", None, None),
        P(),
        P(),
        P(None, "dp"),
        P(None, "dp"),
        P(None, "dp"),
    )
    out_specs = (P("dp", None, None), P(None, "dp"), P(None, "dp"), P(None, "dp"), P())
    return jax.shard_map(
        body, mesh=mesh, in_specs=in_specs, out_specs=out_specs, check_vma=False
    )
```
